256 devices in a mesh: path: 8 (over z_lo, core), shard: 32 (over z_hi, x, y).
Axes of the slice: x: 4, y: 4, z: 8 (z_hi: 2, z_lo: 4; z = z_hi * 4 + z_lo), core: 2. Of those that a mesh axis runs over, the one named last changes fastest.
Arguments:
- tokens: bfloat16 [3072, 2048], P(('path', 'shard')), may hold values from -6 to 6
- routes: int32 [3072, 1], P(('path', 'shard')), may hold values from 0 to 7; in each aligned block of 12 rows (0 to 11, 12 to 23, ...) at most 2 rows name the same one
- cotangent: bfloat16 [3072, 2048], P(('path', 'shard')), may hold values from -6 to 6
- gains: bfloat16 [8, 2, 2048], P('path'), may hold values from 0.099609375 to 1.8984375
- w_in: bfloat16 [8, 2, 2048, 8192], P('path', None, None, 'shard'), may hold values from -0.125 to 0.125
- w_out: bfloat16 [8, 2, 8192, 2048], P('path', None, 'shard'), may hold values from -0.0625 to 0.0625
- partners: int32 [2, 8], replicated, may hold values from 0 to 7, as said below
Outputs:
- delta_in: bfloat16 [8, 2, 2048, 8192], P('path', None, None, 'shard')
- delta_out: bfloat16 [8, 2, 8192, 2048], P('path', None, 'shard')
The draws below stay inside these ranges and needn't reach their ends.
Inputs may be any that keep to these rules, and one draw needn't show every extreme that they name: `routes`: in each device's block of 12 rows at most 2 rows name one path, and some path gets exactly 2 rows of some block. Each row pairs the paths: partners[l, partners[l, p]] = p and partners[l, p] != p.
All inputs are finite; a program needn't handle non-finite values.
Results may differ from the reference program's by a relative error of at most 0.03.
Values may be sent and summed in bfloat16 or wider, within the bound.
A program may use at most 64 MiB of HBM per device.

```python
import math
import jax
import jax.numpy as jnp
import numpy as np
from jax import lax

D = 2048
FF = 8192
SLOTS = 16
LEVELS = 2
TOK_DEV = 12
CAP = 2
PATH_ROWS = 512
TOKENS = 3072
N_PATH = 8
N_SHARD = 32


def draw_partners(key, part):
    rows = []
    for level in range(LEVELS):
        order = jax.random.permutation(jax.random.fold_in(key, 17 + level), N_PATH).astype(jnp.int32)
        pairs = order.reshape(N_PATH // 2, 2)
        mate = jnp.zeros((N_PATH,), jnp.int32)
        mate = mate.at[pairs[:, 0]].set(pairs[:, 1])
        mate = mate.at[pairs[:, 1]].set(pairs[:, 0])
        rows.append(mate)
    return jnp.stack(rows)


def levels(stream_key, shape, shards, least, largest):
    factor_of, own = 1.0, jax.random.fold_in(stream_key, 6)
    for position, blocks in shards:
        draws = jnp.exp(jax.random.uniform(jax.random.fold_in(own, position), (blocks,), jnp.float32, least / len(shards), largest / len(shards)))
        factor_of = factor_of * jnp.repeat(draws, shape[position] // blocks).reshape([-1 if axis == position else 1 for axis in range(len(shape))])
    return factor_of


def deal_out(key, own, number, rows, count, top, reach, lean):
    ranking = jax.random.permutation(key, count)
    heavy_load, usual = shares(count, rows * top, reach, lean, True), shares(count, rows * top, reach, lean, False)
    places = jnp.arange(count)

    def named(sizes, offset_by):
        used = int((sizes > 0).sum())
        fixed = max(1, used // 4)
        shifted = fixed + (places - fixed + offset_by * (used - fixed)) % max(1, count - fixed)
        return jnp.zeros((count,), jnp.int32).at[ranking[jnp.where(places < fixed, places, shifted)]].set(jnp.asarray(sizes, jnp.int32))

    sizes = jnp.where(number % 4 == 0, named(heavy_load, number // 4), named(usual, number - number // 4 - 1))
    mixed = jax.random.permutation(jax.random.fold_in(own, 3), count)
    donor, taker = mixed[0:count // 2 * 2:2], mixed[1:count // 2 * 2:2]
    room = jnp.minimum(sizes[donor] - 1, reach - sizes[taker]) // 2
    room = jnp.where((donor == ranking[0]) | (taker == ranking[0]) | (sizes[taker] == 0), 0, jnp.maximum(room, 0))
    shifted = jax.random.randint(jax.random.fold_in(own, 4), (count // 2,), 0, 1 << 20) % (room + 1)
    sizes = sizes.at[donor].add(-shifted).at[taker].add(shifted)
    items = jnp.searchsorted(jnp.cumsum(sizes), jnp.arange(rows * top), side="right").astype(jnp.int32)
    grid = items.reshape(top, rows).T
    grid = grid[jax.random.permutation(jax.random.fold_in(own, 1), rows)]
    offset_by = jax.random.randint(jax.random.fold_in(own, 2), (rows, 1), 0, top)
    return jnp.take_along_axis(grid, (jnp.arange(top)[None, :] + offset_by) % top, axis=1)


def shares(amount, total, limit, skew, full):
    weights = [(1 << 20) // math.isqrt(standing ** skew) + 1 for standing in range(1, amount + 1)]
    largest = limit if full else min(limit, max(-(-total // amount), total * weights[0] // sum(weights)))
    least = 1 if total - largest >= amount - 1 else 0
    holding, rest = [largest] + [least] * (amount - 1), total - largest - least * (amount - 1)
    while rest > 0:
        movable = [i for i in range(1, amount) if holding[i] < largest] or [i for i in range(1, amount) if holding[i] < limit]
        mass, budget = sum([weights[i] for i in movable]), rest
        for i in movable:
            more = min(limit - holding[i], max(1, budget * weights[i] // mass), rest)
            holding[i] = holding[i] + more
            rest = rest - more
    return np.array(holding)


def normal_values(stream_key, dims, width, limit, shards=(), held_as=jnp.bfloat16):
    drawn = width * jax.random.normal(stream_key, dims, jnp.float32)
    if shards:
        drawn = drawn * levels(stream_key, dims, shards, -0.22, 0.18)
    return jnp.clip(drawn, -limit, limit).astype(held_as)


def setup_inputs(seed: int = 0) -> dict:
    streams_of = jax.random.split(jax.random.key(seed), 8)
    tokens = normal_values(streams_of[0], (TOKENS, D), 1.0, 6.0, ((0, 256),))
    routes_keys = jax.random.split(jax.random.fold_in(streams_of[1], 1), TOKENS // TOK_DEV)
    routes_turns = jax.random.permutation(jax.random.fold_in(streams_of[1], 3), TOKENS // TOK_DEV)
    routes = jax.vmap(lambda own, number: deal_out(jax.random.fold_in(streams_of[1], 2), own, number, TOK_DEV, N_PATH, 1, CAP, 2))(routes_keys, routes_turns).reshape((TOKENS, 1))
    cotangent = normal_values(streams_of[2], (TOKENS, D), 1.0, 6.0, ((0, 256),))
    gains = jnp.clip(1.0 + 0.18 * jax.random.normal(streams_of[3], (N_PATH, LEVELS, D), jnp.float32), 0.099609375, 1.8984375).astype(jnp.bfloat16)
    w_in = normal_values(streams_of[4], (N_PATH, LEVELS, D, FF), D ** -0.5, 0.125, ((0, 8), (3, 32)))
    w_out = normal_values(streams_of[5], (N_PATH, LEVELS, FF, D), FF ** -0.5, 0.0625, ((0, 8), (2, 32)))
    partners = draw_partners(jax.random.fold_in(streams_of[7], 71), 0)
    return {"tokens": tokens, "routes": routes, "cotangent": cotangent, "gains": gains, "w_in": w_in, "w_out": w_out, "partners": partners}


def norm_value(v, gain):
    return v * lax.rsqrt(lax.optimization_barrier(jnp.mean(v * v, axis=-1, keepdims=True)) + 1e-05) * gain.astype(jnp.float32)

def norm_pull(h, gain, grad):

    def value(v):
        return norm_value(v, gain)
    return jax.vjp(value, h.astype(jnp.float32))[1](grad)[0]

def gelu_pull(pre, grad):
    return jax.vjp(jax.nn.gelu, pre)[1](grad)[0]

def grouped(left, right_t):
    rows = left.shape[0]
    left3 = left.astype(jnp.float32).reshape(rows, N_SHARD, -1)
    right3 = right_t.astype(jnp.float32).reshape(N_SHARD, left3.shape[2], -1)
    parts = jnp.einsum('rsf,sfd->srd', left3, right3).astype(jnp.bfloat16)
    return lax.optimization_barrier(jnp.sum(parts.astype(jnp.float32), axis=0))

def one_path(inputs):
    x, dy, gain, wi, wo = inputs
    n1 = norm_value(x.astype(jnp.float32), gain[0]).astype(jnp.bfloat16)
    a1 = jnp.dot(n1, wi[0], preferred_element_type=jnp.float32)
    u1 = jax.nn.gelu(a1).astype(jnp.bfloat16)
    y1 = grouped(u1, wo[0])
    h1 = (x.astype(jnp.float32) + y1).astype(jnp.bfloat16)
    n2 = norm_value(h1.astype(jnp.float32), gain[1]).astype(jnp.bfloat16)
    a2 = jnp.dot(n2, wi[1], preferred_element_type=jnp.float32)
    u2 = jax.nn.gelu(a2).astype(jnp.bfloat16)
    g_out2 = jnp.dot(u2.T, dy, preferred_element_type=jnp.float32)
    du2 = jnp.dot(dy, wo[1].T, preferred_element_type=jnp.float32)
    da2 = gelu_pull(a2, du2).astype(jnp.bfloat16)
    g_in2 = jnp.dot(n2.T, da2, preferred_element_type=jnp.float32)
    dn2 = grouped(da2, wi[1].T)
    dh1 = (dy.astype(jnp.float32) + norm_pull(h1, gain[1], dn2)).astype(jnp.bfloat16)
    g_out1 = jnp.dot(u1.T, dh1, preferred_element_type=jnp.float32)
    du1 = jnp.dot(dh1, wo[0].T, preferred_element_type=jnp.float32)
    da1 = gelu_pull(a1, du1).astype(jnp.bfloat16)
    g_in1 = jnp.dot(n1.T, da1, preferred_element_type=jnp.float32)
    return (jnp.stack([g_in1, g_in2]), jnp.stack([g_out1, g_out2]))

def reference(tokens, routes, cotangent, gains, w_in, w_out, partners):
    route = routes[:, 0].reshape(N_PATH, N_SHARD, TOK_DEV)
    order = jnp.arange(TOK_DEV, dtype=jnp.int32)
    same = (route[..., :, None] == route[..., None, :]) & (order[None, :] < order[:, None])
    rank = lax.optimization_barrier(jnp.sum(same.astype(jnp.int32), axis=-1))
    shard_ix = jnp.arange(N_SHARD, dtype=jnp.int32)[None, :, None]
    source = jnp.arange(N_PATH, dtype=jnp.int32)[:, None, None]
    place = (route * PATH_ROWS + shard_ix * SLOTS + source * CAP + rank).reshape(-1).astype(jnp.int32)
    x = jnp.zeros((N_PATH * PATH_ROWS, D), jnp.bfloat16).at[place].set(tokens).reshape(N_PATH, PATH_ROWS, D)
    dy = jnp.zeros((N_PATH * PATH_ROWS, D), jnp.bfloat16).at[place].set(cotangent).reshape(N_PATH, PATH_ROWS, D)
    g_in, g_out = lax.map(one_path, (x, dy, gains, w_in, w_out))
    scale = 1.0 / jnp.sqrt(jnp.float32(PATH_ROWS))
    e_in = (-g_in * scale).astype(jnp.bfloat16)
    e_out = (-g_out * scale).astype(jnp.bfloat16)
    outs_in = []
    outs_out = []
    for level in range(LEVELS):
        mate = partners[level]
        own_in = e_in[:, level].astype(jnp.float32)
        own_out = e_out[:, level].astype(jnp.float32)
        outs_in.append(((own_in + own_in[mate]) * 0.5).astype(jnp.bfloat16))
        outs_out.append(((own_out + own_out[mate]) * 0.5).astype(jnp.bfloat16))
    return (jnp.stack(outs_in, axis=1), jnp.stack(outs_out, axis=1))
```

```python
import functools

import jax
import jax.numpy as jnp
from jax import lax
from jax.experimental import pallas as pl
from jax.experimental.pallas import tpu as pltpu
from jax.sharding import PartitionSpec as P

SLOTS = 16
MESH = pl.DeviceIdType.MESH
BF = jnp.bfloat16
F32 = jnp.float32
HALF = 1024
QUARTER = 512


class Wires:
    def __init__(self, send, recv):
        self.send, self.recv, self.made = send, recv, []
        shard = lax.axis_index("shard")
        self.zh = shard // 16
        self.x = lax.rem(shard // 4, 4)
        self.y = lax.rem(shard, 4)

    def shard(self, zh, x, y):
        return {"shard": zh * 16 + x * 4 + y}

    def xs(self, step):
        return lax.rem(self.x + step + 4, 4)

    def ys(self, step):
        return lax.rem(self.y + step + 4, 4)

    def pos(self, axis, step):
        return self.xs(step) if axis == "x" else self.ys(step)

    def beside(self, axis, step):
        if axis == "x":
            return self.shard(self.zh, self.xs(step), self.y)
        return self.shard(self.zh, self.x, self.ys(step))

    def across(self):
        return self.shard(1 - self.zh, self.x, self.y)

    def push(self, src, dst, to):
        k = len(self.made)
        copy = pltpu.make_async_remote_copy(
            src_ref=src,
            dst_ref=dst,
            send_sem=self.send.at[k],
            recv_sem=self.recv.at[k],
            device_id=to,
            device_id_type=MESH,
        )
        copy.start()
        self.made.append(copy)
        return copy

    def drain(self):
        for copy in self.made:
            copy.wait_send()

    def greet(self):
        barrier = pltpu.get_barrier_semaphore()
        for to in (
            self.beside("x", 1),
            self.beside("x", -1),
            self.beside("y", 1),
            self.beside("y", -1),
            self.across(),
        ):
            pl.semaphore_signal(barrier, inc=1, device_id=to, device_id_type=MESH)
        pl.semaphore_wait(barrier, 5)


def run(*tasks):
    tasks = list(tasks)
    while tasks:
        for task in list(tasks):
            try:
                next(task)
            except StopIteration:
                tasks.remove(task)


def ring_gather(w, axis, view, low, size):
    here, left, right = w.pos(axis, 0), w.pos(axis, -1), w.pos(axis, 1)
    own = view(here, low, size)
    go_right = w.push(own, own, w.beside(axis, 1))
    go_left = w.push(own, own, w.beside(axis, -1))
    yield
    go_right.wait_recv()
    part = view(left, low, size // 2)
    on_right = w.push(part, part, w.beside(axis, 1))
    yield
    go_left.wait_recv()
    part = view(right, low + size // 2, size // 2)
    on_left = w.push(part, part, w.beside(axis, -1))
    yield
    on_right.wait_recv()
    on_left.wait_recv()


def gather(w, full):
    own = full.at[w.zh, w.x, w.y]
    over = w.push(own, own, w.across())

    def half(plane, first, second, low, wait):
        if wait:
            yield
            over.wait_recv()

        def line(i, start, size):
            cols = pl.ds(start, size)
            if first == "x":
                return full.at[plane, i, w.y, :, cols]
            return full.at[plane, w.x, i, :, cols]

        def sheet(i, start, size):
            cols = pl.ds(start, size)
            if second == "x":
                return full.at[plane, i, :, :, cols]
            return full.at[plane, :, i, :, cols]

        yield from ring_gather(w, first, line, low, HALF)
        yield from ring_gather(w, second, sheet, low, HALF)

    waited = []

    def other(first, second, low):
        yield
        if not waited:
            over.wait_recv()
            waited.append(True)
        yield from half(1 - w.zh, first, second, low, False)

    return [
        half(w.zh, "x", "y", 0, False),
        half(w.zh, "y", "x", HALF, False),
        other("x", "y", 0),
        other("y", "x", HALF),
    ]


def ring_reduce(w, axis, view, low, bufs, out):
    from_left, from_right, in_r_lo, in_r_hi, in_l_lo, in_l_hi, tmp_r, tmp_l = bufs
    q = QUARTER
    here, left, right, far = (w.pos(axis, s) for s in (0, -1, 1, 2))
    to_right, to_left = w.beside(axis, 1), w.beside(axis, -1)
    a = w.push(view(far, low, q), from_left, to_right)
    b = w.push(view(far, low + q, q), from_right, to_left)
    c = w.push(view(right, low + q, q), in_r_hi, to_right)
    d = w.push(view(left, low, q), in_l_lo, to_left)
    yield
    a.wait_recv()
    tmp_r[...] = (view(right, low, q)[...].astype(F32) + from_left[...].astype(F32)).astype(BF)
    e = w.push(tmp_r, in_r_lo, to_right)
    yield
    b.wait_recv()
    tmp_l[...] = (view(left, low + q, q)[...].astype(F32) + from_right[...].astype(F32)).astype(BF)
    f = w.push(tmp_l, in_l_hi, to_left)
    yield
    c.wait_recv()
    f.wait_recv()
    hi = (
        view(here, low + q, q)[...].astype(F32)
        + in_r_hi[...].astype(F32)
        + in_l_hi[...].astype(F32)
    )
    out(1, hi)
    yield
    d.wait_recv()
    e.wait_recv()
    lo = view(here, low, q)[...].astype(F32) + in_r_lo[...].astype(F32) + in_l_lo[...].astype(F32)
    out(0, lo)


def reduce(w, part, big, small, mid, far, near, total):
    over = {}

    def half(k, plane, mine, first, second, low):
        def sheet(i, start, size):
            cols = pl.ds(start, size)
            if first == "x":
                return part.at[plane, i, :, :, cols]
            return part.at[plane, :, i, :, cols]

        def keep(which, value):
            mid[k, :, :, pl.ds(which * QUARTER, QUARTER)] = value.astype(BF)

        def line(i, start, size):
            return mid.at[k, i, :, pl.ds(start, size)]

        def last(which, value):
            cols = pl.ds(low + which * QUARTER, QUARTER)
            if mine:
                total[:, cols] = value
            else:
                far[:, cols] = value.astype(BF)

        yield from ring_reduce(w, first, sheet, low, [big.at[k, n] for n in range(8)], keep)
        yield from ring_reduce(w, second, line, 0, [small.at[k, n] for n in range(8)], last)
        if not mine:
            cols = pl.ds(low, HALF)
            over[low] = w.push(far.at[:, cols], near.at[:, cols], w.across())

    def finish():
        for low in (0, HALF):
            over[low].wait_recv()
            cols = pl.ds(low, HALF)
            total[:, cols] = total[:, cols] + near[:, cols].astype(F32)

    tasks = [
        half(0, 1 - w.zh, False, "x", "y", 0),
        half(1, 1 - w.zh, False, "y", "x", HALF),
        half(2, w.zh, True, "x", "y", 0),
        half(3, w.zh, True, "y", "x", HALF),
    ]
    return tasks, finish


def reduce_scratch():
    return [
        pltpu.VMEM((4, 8, 4, SLOTS, QUARTER), BF),
        pltpu.VMEM((4, 8, SLOTS, QUARTER), BF),
        pltpu.VMEM((4, 4, SLOTS, HALF), BF),
        pltpu.VMEM((SLOTS, 2 * HALF), BF),
        pltpu.VMEM((SLOTS, 2 * HALF), BF),
    ]


def gather_kernel(count, *refs):
    owns, fulls, send, recv = refs[:count], refs[count : 2 * count], refs[-2], refs[-1]
    w = Wires(send, recv)
    for own, full in zip(owns, fulls):
        full[w.zh, w.x, w.y] = own[...]
    w.greet()
    tasks = []
    for full in fulls:
        tasks += gather(w, full)
    run(*tasks)
    w.drain()


def reduce_kernel(part, total, big, small, mid, far, near, send, recv):
    w = Wires(send, recv)
    w.greet()
    tasks, finish = reduce(w, part, big, small, mid, far, near, total)
    run(*tasks)
    finish()
    w.drain()


def vmem():
    return pl.BlockSpec(memory_space=pltpu.VMEM)


def gather_call(number, *owns):
    count = len(owns)
    width = owns[0].shape[1]
    got = pl.pallas_call(
        functools.partial(gather_kernel, count),
        out_shape=[jax.ShapeDtypeStruct((2, 4, 4, SLOTS, width), BF)] * count,
        in_specs=[vmem()] * count,
        out_specs=[vmem()] * count,
        scratch_shapes=[pltpu.SemaphoreType.DMA((33 * count,)), pltpu.SemaphoreType.DMA((33 * count,))],
        compiler_params=pltpu.CompilerParams(
            collective_id=number, has_side_effects=True, vmem_limit_bytes=40 << 20
        ),
    )(*owns)
    return [full.reshape(512, width) for full in got]


def reduce_call(number, part):
    width = part.shape[1]
    return pl.pallas_call(
        reduce_kernel,
        out_shape=jax.ShapeDtypeStruct((SLOTS, width), F32),
        in_specs=[vmem()],
        out_specs=vmem(),
        scratch_shapes=reduce_scratch()
        + [pltpu.SemaphoreType.DMA((50,)), pltpu.SemaphoreType.DMA((50,))],
        compiler_params=pltpu.CompilerParams(
            collective_id=number, has_side_effects=True, vmem_limit_bytes=40 << 20
        ),
    )(part.reshape(2, 4, 4, SLOTS, width))


def norm_value(v, gain):
    return v * lax.rsqrt(jnp.mean(v * v, axis=-1, keepdims=True) + 1e-05) * gain.astype(jnp.float32)


def norm_pull(h, gain, grad):

    def value(v):
        return norm_value(v, gain)

    return jax.vjp(value, h.astype(jnp.float32))[1](grad)[0]


def gelu_pull(pre, grad):
    return jax.vjp(jax.nn.gelu, pre)[1](grad)[0]


def pair_mean(piece, table):
    paths = table.shape[0]
    pick = (table[:, None] == jnp.arange(paths, dtype=jnp.int32)[None, :]).astype(jnp.float32)
    values = piece.astype(jnp.float32)
    other = jnp.einsum("pq,qrc->prc", pick, values, precision=lax.Precision.HIGHEST)
    return ((values + other) * 0.5).astype(jnp.bfloat16)


def body(tokens, routes, cotangent, gains, w_in, w_out, partners):
    paths = lax.axis_size("path")
    slots = SLOTS
    cap = slots // paths
    width = tokens.shape[1]
    route = routes[:, 0]
    order = jnp.arange(route.shape[0], dtype=jnp.int32)
    same = (route[:, None] == route[None, :]) & (order[None, :] < order[:, None])
    rank = jnp.sum(same.astype(jnp.int32), axis=1)
    target = route * cap + rank
    select = (jnp.arange(slots, dtype=jnp.int32)[:, None] == target[None, :]).astype(jnp.bfloat16)
    packed_x = (
        jnp.dot(select, tokens, preferred_element_type=jnp.float32)
        .astype(jnp.bfloat16)
        .reshape(paths, cap, width)
    )
    packed_dy = (
        jnp.dot(select, cotangent, preferred_element_type=jnp.float32)
        .astype(jnp.bfloat16)
        .reshape(paths, cap, width)
    )
    got_x, got_dy = (
        lax.all_to_all(packed_x, "path", split_axis=0, concat_axis=0, tiled=True),
        lax.all_to_all(packed_dy, "path", split_axis=0, concat_axis=0, tiled=True),
    )
    own_x = got_x.reshape(slots, width)
    own_dy = got_dy.reshape(slots, width)
    own_n1 = norm_value(own_x.astype(jnp.float32), gains[0, 0]).astype(jnp.bfloat16)
    n1, full_dy = gather_call(0, own_n1, own_dy)
    gain_high = gains[0, 1]
    wi_low = w_in[0, 0]
    wi_high = w_in[0, 1]
    wo_low = w_out[0, 0]
    wo_high = w_out[0, 1]
    hidden = wi_low.shape[1]
    scale = 1.0 / jnp.sqrt(jnp.float32(n1.shape[0]))
    a1 = jnp.dot(n1, wi_low, preferred_element_type=jnp.float32)
    u1 = jax.nn.gelu(a1).astype(jnp.bfloat16)
    part_low = jnp.dot(u1, wo_low, preferred_element_type=jnp.float32)
    mixed_own = reduce_call(1, part_low.astype(jnp.bfloat16))
    h_own = (own_x.astype(jnp.float32) + mixed_own).astype(jnp.bfloat16)
    own_n2 = norm_value(h_own.astype(jnp.float32), gain_high).astype(jnp.bfloat16)
    (n2,) = gather_call(2, own_n2)
    a2 = jnp.dot(n2, wi_high, preferred_element_type=jnp.float32)
    u2 = jax.nn.gelu(a2).astype(jnp.bfloat16)
    g_out2 = jnp.dot(u2.T, full_dy, preferred_element_type=jnp.float32)
    du2 = jnp.dot(full_dy, wo_high.T, preferred_element_type=jnp.float32)
    da2 = gelu_pull(a2, du2).astype(jnp.bfloat16)
    g_in2 = jnp.dot(n2.T, da2, preferred_element_type=jnp.float32)
    part_back = jnp.dot(da2, wi_high.T, preferred_element_type=jnp.float32)
    e_in2 = (-g_in2 * scale).astype(jnp.bfloat16).reshape(paths, width // paths, hidden)
    e_out2 = (-g_out2 * scale).astype(jnp.bfloat16).reshape(paths, width // paths, hidden)
    back_own = reduce_call(3, part_back.astype(jnp.bfloat16))
    dh_own = (own_dy.astype(jnp.float32) + norm_pull(h_own, gain_high, back_own)).astype(
        jnp.bfloat16
    )
    (full_dh,) = gather_call(4, dh_own)
    g_out1 = jnp.dot(u1.T, full_dh, preferred_element_type=jnp.float32)
    du1 = jnp.dot(full_dh, wo_low.T, preferred_element_type=jnp.float32)
    da1 = gelu_pull(a1, du1).astype(jnp.bfloat16)
    g_in1 = jnp.dot(n1.T, da1, preferred_element_type=jnp.float32)
    e_in1 = (-g_in1 * scale).astype(jnp.bfloat16).reshape(paths, width // paths, hidden)
    e_out1 = (-g_out1 * scale).astype(jnp.bfloat16).reshape(paths, width // paths, hidden)
    avg_in1 = lax.all_to_all(
        pair_mean(
            lax.all_to_all(e_in1, "path", split_axis=0, concat_axis=0, tiled=True), partners[0]
        ),
        "path",
        split_axis=0,
        concat_axis=0,
        tiled=True,
    )
    avg_out1 = lax.all_to_all(
        pair_mean(
            lax.all_to_all(e_out1, "path", split_axis=0, concat_axis=0, tiled=True), partners[0]
        ),
        "path",
        split_axis=0,
        concat_axis=0,
        tiled=True,
    )
    avg_in2 = lax.all_to_all(
        pair_mean(
            lax.all_to_all(e_in2, "path", split_axis=0, concat_axis=0, tiled=True), partners[1]
        ),
        "path",
        split_axis=0,
        concat_axis=0,
        tiled=True,
    )
    avg_out2 = lax.all_to_all(
        pair_mean(
            lax.all_to_all(e_out2, "path", split_axis=0, concat_axis=0, tiled=True), partners[1]
        ),
        "path",
        split_axis=0,
        concat_axis=0,
        tiled=True,
    )
    delta_in = jnp.stack([avg_in1.reshape(width, hidden), avg_in2.reshape(width, hidden)])[None]
    delta_out = jnp.stack([avg_out1.reshape(hidden, width), avg_out2.reshape(hidden, width)])[None]
    return (delta_in, delta_out)


def solution(mesh):
    in_specs = (
        P(("path", "shard"), None),
        P(("path", "shard"), None),
        P(("path", "shard"), None),
        P("path", None, None),
        P("path", None, None, "shard"),
        P("path", None, "shard", None),
        P(),
    )
    out_specs = (P("path", None, None, "shard"), P("path", None, "shard", None))
    return jax.shard_map(body, mesh=mesh, in_specs=in_specs, out_specs=out_specs, check_vma=False)
```

```python
import jax
import jax.numpy as jnp
from jax import lax
from jax.experimental import pallas as pl
from jax.experimental.pallas import tpu as pltpu
from jax.sharding import PartitionSpec as P

SLOTS = 16
MESH = pl.DeviceIdType.MESH
BF = jnp.bfloat16
F32 = jnp.float32
WIDTH = 2048
HALF = 1024
QUARTER = 512
HIDDEN = 256
ROWS = 512
PLANE = 256
COPIES = 420
RATE = 90000.0
DELAY = 2.5
SIDE_LAG = 3.0


class Wires:
    def __init__(self, plan, send, recv):
        self.plan, self.send, self.recv, self.made = plan, send, recv, []
        path = lax.axis_index("path")
        self.path = path
        self.zl, self.core = path // 2, lax.rem(path, 2)
        self.z_two = lax.rem(self.zl + 2, 4)
        self.z_one = self.zl + 1 - 2 * lax.rem(self.zl, 2)
        self.z_three = lax.rem(self.z_one + 2, 4)
        shard = lax.axis_index("shard")
        self.zh = shard // 16
        self.x = lax.rem(shard // 4, 4)
        self.y = lax.rem(shard, 4)

    def shard(self, zh, x, y):
        return {"shard": zh * 16 + x * 4 + y}

    def xs(self, step):
        return lax.rem(self.x + step + 4, 4)

    def ys(self, step):
        return lax.rem(self.y + step + 4, 4)

    def pos(self, axis, step):
        return self.xs(step) if axis == "x" else self.ys(step)

    def beside(self, axis, step):
        if axis == "x":
            to = self.shard(self.zh, self.xs(step), self.y)
        else:
            to = self.shard(self.zh, self.x, self.ys(step))
        ways = {1: "+", -1: "-", 2: "+-"}[step]
        return to, [(axis + way, 2.0) for way in ways]

    def across(self):
        return self.shard(1 - self.zh, self.x, self.y), [("z", 4.0), ("far", 0.0)]

    def level_with(self, z, load):
        return {"path": z * 2 + self.core}, [("z", load)]

    def sibling(self):
        return {"path": self.zl * 2 + 1 - self.core}, [("core", 0.4)]

    def peers(self):
        for dz in range(4):
            for dc in range(2):
                if dz or dc:
                    core = lax.rem(self.core + dc, 2)
                    yield lax.rem(self.zl + dz, 4) * 2 + core

    def push(self, src, dst, where):
        to, links = where
        k = len(self.made)
        copy = pltpu.make_async_remote_copy(
            src_ref=src,
            dst_ref=dst,
            send_sem=self.send.at[k],
            recv_sem=self.recv.at[k],
            device_id=to,
            device_id_type=MESH,
        )
        copy.start()
        size = 2
        for extent in src.shape:
            size *= extent
        self.made.append(copy)
        self.plan.sent(copy, size, links)
        return copy

    def drain(self):
        for copy in self.made:
            copy.wait_send()

    def greet(self, meanwhile):
        barrier = pltpu.get_barrier_semaphore()
        peers = [self.beside(axis, step)[0] for axis in "xy" for step in (1, -1, 2)]
        peers += [self.across()[0]] + [{"path": to} for to in self.peers()]
        for to in peers:
            pl.semaphore_signal(barrier, inc=1, device_id=to, device_id_type=MESH)
        meanwhile()
        pl.semaphore_wait(barrier, len(peers))


class Plan:
    def __init__(self):
        self.clock, self.free, self.due, self.marks = 0.0, {}, {}, {}

    def sent(self, copy, size, links):
        end = self.clock
        for name, load in links:
            if name == "far":
                end += 1.5
                continue
            start = max(self.clock, self.free.get(name, 0.0))
            self.free[name] = start + size * load / RATE
            end = max(end, self.free[name])
        self.due[id(copy)] = end + DELAY
        self.clock += 0.08

    def work(self, time):
        self.clock += time

    def mark(self, name):
        self.marks.setdefault(name, []).append(self.clock)

    def need(self, *names):
        yield "marks", names

    def ready(self, state):
        kind, items = state
        if kind == "copies":
            return max(self.due[id(copy)] for copy in items)
        times = [0.0]
        for name, count in items:
            have = self.marks.get(name, [])
            if len(have) < count:
                return None
            times.append(have[count - 1])
        return max(times)

    def run(self, tasks):
        tasks = [[lag, task, None] for lag, task in tasks]
        for entry in tasks:
            entry[2] = next(entry[1])
        while tasks:
            best = None
            for entry in tasks:
                time = self.ready(entry[2])
                if time is None:
                    continue
                time = max(time + entry[0], self.clock)
                if best is None or time < best[0] - 1e-6:
                    best = (time, entry)
            time, entry = best
            self.clock = max(self.clock, self.ready(entry[2]))
            try:
                entry[2] = next(entry[1])
            except StopIteration:
                tasks.remove(entry)


def ring_gather(w, axis, view, low, size):
    here, left, right = w.pos(axis, 0), w.pos(axis, -1), w.pos(axis, 1)
    own = view(here, low, size)
    go_right = w.push(own, own, w.beside(axis, 1))
    go_left = w.push(own, own, w.beside(axis, -1))
    yield "copies", [go_right]
    go_right.wait_recv()
    part = view(left, low, size // 2)
    on_right = w.push(part, part, w.beside(axis, 1))
    yield "copies", [go_left]
    go_left.wait_recv()
    part = view(right, low + size // 2, size // 2)
    on_left = w.push(part, part, w.beside(axis, -1))
    yield "copies", [on_right, on_left]
    on_right.wait_recv()
    on_left.wait_recv()


def ring_share(w, axis, view, low, size):
    own = view(w.pos(axis, 0), low, size)
    sent = [w.push(own, own, w.beside(axis, step)) for step in (1, -1, 2)]
    yield "copies", sent
    for copy in sent:
        copy.wait_recv()


def gather(w, plan, full, name, after):
    over, waited = [], []

    def half(mine, first, second, low):
        plane = w.zh if mine else 1 - w.zh
        yield from plan.need(*after)
        if not over:
            own = full.at[w.zh, w.x, w.y]
            over.append(w.push(own, own, w.across()))
        if not mine:
            yield "copies", over
            if not waited:
                over[0].wait_recv()
                waited.append(True)

        def line(i, start, size):
            cols = pl.ds(start, size)
            if first == "x":
                return full.at[plane, i, w.y, :, cols]
            return full.at[plane, w.x, i, :, cols]

        def sheet(i, start, size):
            cols = pl.ds(start, size)
            if second == "x":
                return full.at[plane, i, :, :, cols]
            return full.at[plane, :, i, :, cols]

        yield from ring_share(w, first, line, low, HALF)
        yield from ring_gather(w, second, sheet, low, HALF)
        plan.mark((name, mine))

    return [
        half(True, "x", "y", 0),
        half(True, "y", "x", HALF),
        half(False, "x", "y", 0),
        half(False, "y", "x", HALF),
    ]


def path_gather(w, plan, view, name, after):
    def block(z):
        return view(z * 2 + w.core)

    yield from plan.need(*after)
    own = block(w.zl)
    two = w.push(own, own, w.level_with(w.z_two, 4.0))
    one = w.push(own, own, w.level_with(w.z_one, 2.0))
    aside = [w.push(own, own, w.sibling())]
    yield "copies", [two]
    two.wait_recv()
    got = block(w.z_two)
    three = w.push(got, got, w.level_with(w.z_one, 2.0))
    aside.append(w.push(got, got, w.sibling()))
    yield "copies", [one]
    one.wait_recv()
    got = block(w.z_one)
    aside.append(w.push(got, got, w.sibling()))
    yield "copies", [three]
    three.wait_recv()
    got = block(w.z_three)
    aside.append(w.push(got, got, w.sibling()))
    yield "copies", aside
    for copy in aside:
        copy.wait_recv()
    plan.mark(name)


def ring_reduce(w, axis, view, low, bufs, out):
    from_left, from_right, in_r_lo, in_r_hi, in_l_lo, in_l_hi, tmp_r, tmp_l = bufs
    q = QUARTER
    here, left, right, far = (w.pos(axis, s) for s in (0, -1, 1, 2))
    to_right, to_left = w.beside(axis, 1), w.beside(axis, -1)
    a = w.push(view(far, low, q), from_left, to_right)
    b = w.push(view(far, low + q, q), from_right, to_left)
    c = w.push(view(right, low + q, q), in_r_hi, to_right)
    d = w.push(view(left, low, q), in_l_lo, to_left)
    yield "copies", [a]
    a.wait_recv()
    tmp_r[...] = (view(right, low, q)[...].astype(F32) + from_left[...].astype(F32)).astype(BF)
    w.plan.work(0.2)
    e = w.push(tmp_r, in_r_lo, to_right)
    yield "copies", [b]
    b.wait_recv()
    tmp_l[...] = (view(left, low + q, q)[...].astype(F32) + from_right[...].astype(F32)).astype(BF)
    w.plan.work(0.2)
    f = w.push(tmp_l, in_l_hi, to_left)
    yield "copies", [c, d, e, f]
    for copy in (c, d, e, f):
        copy.wait_recv()
    out(0, view(here, low, q)[...].astype(F32) + in_r_lo[...].astype(F32) + in_l_lo[...].astype(F32))
    out(
        1,
        view(here, low + q, q)[...].astype(F32)
        + in_r_hi[...].astype(F32)
        + in_l_hi[...].astype(F32),
    )
    w.plan.work(0.4)


def ring_total(w, axis, view, bufs, out):
    sent = [
        w.push(view(w.pos(axis, step)), buf, w.beside(axis, step))
        for step, buf in zip((1, -1, 2), bufs)
    ]
    yield "copies", sent
    for copy in sent:
        copy.wait_recv()
    value = view(w.pos(axis, 0))[...].astype(F32)
    for buf in bufs:
        value = value + buf[...].astype(F32)
    out(value)
    w.plan.work(0.2)


def reduce(w, plan, part, scratch, name, after):
    big, small, mid, far, near, total = scratch
    over = {}

    def half(k, mine, first, second, low):
        plane = w.zh if mine else 1 - w.zh
        yield from plan.need(((after, mine), 1))

        def sheet(i, start, size):
            cols = pl.ds(start, size)
            if first == "x":
                return part.at[plane, i, :, :, cols]
            return part.at[plane, :, i, :, cols]

        def keep(which, value):
            mid[k, :, :, pl.ds(which * QUARTER, QUARTER)] = value.astype(BF)

        def line(i):
            return mid.at[k, i]

        def last(value):
            cols = pl.ds(low, HALF)
            if mine:
                total[:, cols] = value
            else:
                far[:, cols] = value.astype(BF)

        yield from ring_reduce(w, first, sheet, low, [big.at[k, n] for n in range(8)], keep)
        yield from ring_total(w, second, line, [small.at[k, n] for n in range(3)], last)
        if not mine:
            cols = pl.ds(low, HALF)
            over[low] = w.push(far.at[:, cols], near.at[:, cols], w.across())
        plan.mark(name + "_part")

    def finish():
        yield from plan.need((name + "_part", 4))
        yield "copies", [over[0], over[HALF]]
        for low in (0, HALF):
            over[low].wait_recv()
            cols = pl.ds(low, HALF)
            total[:, cols] = total[:, cols] + near[:, cols].astype(F32)
        plan.mark(name)

    return [
        half(0, False, "x", "y", 0),
        half(1, False, "y", "x", HALF),
        half(2, True, "x", "y", 0),
        half(3, True, "y", "x", HALF),
        finish(),
    ]


def reduce_scratch():
    return [
        pltpu.VMEM((4, 8, 4, SLOTS, QUARTER), BF),
        pltpu.VMEM((4, 3, SLOTS, HALF), BF),
        pltpu.VMEM((4, 4, SLOTS, HALF), BF),
        pltpu.VMEM((SLOTS, WIDTH), BF),
        pltpu.VMEM((SLOTS, WIDTH), BF),
        pltpu.VMEM((SLOTS, WIDTH), F32),
    ]


def norm_rows(v, gain):
    return v * lax.rsqrt(jnp.mean(v * v, axis=-1, keepdims=True) + 1e-05) * gain.astype(F32)


def norm_pull(v, gain, grad):
    turn = lax.rsqrt(jnp.mean(v * v, axis=-1, keepdims=True) + 1e-05)
    scaled = grad * gain.astype(F32)
    along = jnp.mean(scaled * v, axis=-1, keepdims=True)
    return turn * scaled - v * (turn * turn * turn * along)


def gelu_both(a):
    c = 0.7978845608028654
    square = a * a
    t = jnp.tanh(c * (a + 0.044715 * a * square))
    value = 0.5 * a * (1.0 + t)
    slope = 0.5 * (1.0 + t) + 0.5 * a * (1.0 - t * t) * (c * (1.0 + 3.0 * 0.044715 * square))
    return value, slope


def dot(a, b):
    return jnp.dot(a, b, preferred_element_type=F32)


def dot_t(a, b):
    return lax.dot_general(a, b, (((1,), (1,)), ((), ())), preferred_element_type=F32)


def step_kernel(
    partners,
    tokens,
    routes,
    cotangent,
    gains,
    w_in,
    w_out,
    d_in,
    d_out,
    packed,
    got,
    x_own,
    dy_own,
    wi,
    wo,
    n1,
    n2,
    dh,
    side,
    n2q,
    dhq,
    r_n1,
    r_dy,
    r_n2,
    r_dh,
    f_u1,
    f_a1,
    f_u2,
    f_a2,
    slope1,
    slope2,
    pull2,
    own_part,
    part1,
    part2,
    *rest,
):
    red1, red2 = rest[0:6], rest[6:12]
    load, send, recv = rest[12:]
    plan = Plan()
    w = Wires(plan, send, recv)
    me = w.path
    mate_low, mate_high = partners[0, me], partners[1, me]
    scale = 1.0 / jnp.sqrt(jnp.float32(ROWS))
    loads = [
        pltpu.make_async_copy(w_in.at[0], wi, load.at[0]),
        pltpu.make_async_copy(w_out.at[0], wo, load.at[1]),
    ]
    for copy in loads:
        copy.start()

    def pack():
        count = tokens.shape[0]
        route = routes[...]
        named = (route == lax.broadcasted_iota(jnp.int32, (count, 128), 1)).astype(BF)
        same = dot_t(named, named)
        before = lax.broadcasted_iota(jnp.int32, same.shape, 1) < lax.broadcasted_iota(
            jnp.int32, same.shape, 0
        )
        rank = jnp.sum(jnp.where(before, same, 0.0), axis=1, keepdims=True)
        place = route.astype(F32) * 2.0 + rank
        slot = lax.broadcasted_iota(jnp.int32, (count, SLOTS), 1).astype(F32)
        select = (place == slot).astype(BF)
        for k, rows in enumerate((tokens, cotangent)):
            sorted_rows = lax.dot_general(
                select, rows[...], (((0,), (0,)), ((), ())), preferred_element_type=F32
            )
            for p in range(8):
                packed[p, k] = sorted_rows[2 * p : 2 * p + 2].astype(BF)

    w.greet(pack)
    hops = [w.push(packed.at[to], got.at[me], ({"path": to}, [("z", 0.0)])) for to in w.peers()]
    got[me] = packed[me]
    for copy in hops:
        copy.wait_recv()
    for p in range(8):
        x_own[2 * p : 2 * p + 2, :] = got[p, 0].astype(F32)
        dy_own[2 * p : 2 * p + 2, :] = got[p, 1].astype(F32)
    rows_n1 = norm_rows(x_own[...], gains[0, 0:1, :]).astype(BF)
    n1[w.zh, w.x, w.y] = rows_n1
    r_n1[me] = rows_n1
    rows_dy = dy_own[...].astype(BF)
    r_dy[me] = rows_dy
    side[w.zh, w.x, w.y, 0:SLOTS] = rows_dy

    def plane_of(mine):
        return w.zh if mine else 1 - w.zh

    def load_weights():
        yield from plan.need()
        for copy in loads:
            copy.wait()
        plan.mark("weights")

    def side_rows():
        yield from plan.need(("r_n1", 1), ("r_dy", 1))
        side[w.zh, w.x, w.y, SLOTS : 2 * SLOTS] = r_n1[mate_low]
        side[w.zh, w.x, w.y, 2 * SLOTS : 3 * SLOTS] = r_dy[mate_high]
        plan.mark("side_rows")

    def first(mine):
        p = plane_of(mine)
        yield from plan.need((("n1", mine), 2), ("weights", 1))
        a = dot(n1[p].reshape(PLANE, WIDTH), wi[0])
        value, slope = gelu_both(a)
        u = value.astype(BF)
        slope1[p] = slope
        f_u1[me, p] = u
        for c in range(0, WIDTH, QUARTER):
            y = dot(u, wo[0, :, c : c + QUARTER]).astype(BF)
            part1[p, :, :, :, c : c + QUARTER] = y.reshape(4, 4, SLOTS, QUARTER)
        plan.work(2.0)
        plan.mark(("part1", mine))
        plan.mark("u1")

    def middle():
        yield from plan.need(("red1", 1))
        h = (x_own[...] + red1[5][...]).astype(BF).astype(F32)
        rows = norm_rows(h, gains[0, 1:2, :]).astype(BF)
        n2[w.zh, w.x, w.y] = rows
        r_n2[me] = rows
        plan.work(0.6)
        plan.mark("n2_own")

    def pull(mine):
        p = plane_of(mine)
        yield from plan.need((("side", mine), 2), ("weights", 1))
        pull2[p] = dot_t(side[p, :, :, 0:SLOTS, :].reshape(PLANE, WIDTH), wo[1])
        plan.work(0.8)
        plan.mark(("pull2", mine))

    def second(mine):
        p = plane_of(mine)
        yield from plan.need((("n2", mine), 2), (("pull2", mine), 1))
        a = dot(n2[p].reshape(PLANE, WIDTH), wi[1])
        value, slope = gelu_both(a)
        f_u2[me, p] = value.astype(BF)
        da = (pull2[p] * slope).astype(BF)
        f_a2[me, p] = da
        for c in range(0, WIDTH, QUARTER):
            y = dot_t(da, wi[1, c : c + QUARTER, :]).astype(BF)
            part2[p, :, :, :, c : c + QUARTER] = y.reshape(4, 4, SLOTS, QUARTER)
        plan.work(2.0)
        plan.mark(("part2", mine))
        plan.mark("u2")

    def side_n2():
        yield from plan.need(("r_n2", 1))
        n2q[w.zh, w.x, w.y] = r_n2[mate_high]
        plan.mark("n2q_own")

    def back():
        yield from plan.need(("red2", 1))
        h = (x_own[...] + red1[5][...]).astype(BF).astype(F32)
        grad = norm_pull(h, gains[0, 1:2, :], red2[5][...])
        rows = (dy_own[...] + grad).astype(BF)
        dh[w.zh, w.x, w.y] = rows
        r_dh[me] = rows
        plan.work(0.8)
        plan.mark("dh_own")

    def side_dh():
        yield from plan.need(("r_dh", 1))
        dhq[w.zh, w.x, w.y] = r_dh[mate_low]
        plan.mark("dhq_own")

    def third(mine):
        p = plane_of(mine)
        yield from plan.need((("dh", mine), 2))
        du = dot_t(dh[p].reshape(PLANE, WIDTH), wo[0])
        f_a1[me, p] = (du * slope1[p]).astype(BF)
        plan.work(0.8)
        plan.mark(("a1", mine))

    def delta(out, level, k, own, mate, own_rows, mate_rows, own_needs, mate_needs, turned):
        def product(factor, rows, cols):
            return (-dot(factor, rows(cols)) * scale).astype(BF)

        def first_part():
            yield from plan.need(*own_needs)
            factor = own[me].reshape(ROWS, HIDDEN).T
            for c in range(0, WIDTH, QUARTER):
                cols = slice(c, c + QUARTER)
                own_part[k, :, cols] = product(factor, own_rows, cols)
                plan.work(0.5)
                yield from plan.need()
            plan.mark(("delta", k))

        def second_part():
            yield from plan.need((("delta", k), 1), *mate_needs)
            factor = own[mate].reshape(ROWS, HIDDEN).T
            for c in range(0, WIDTH, QUARTER):
                cols = slice(c, c + QUARTER)
                there = product(factor, mate_rows, cols).astype(F32)
                mean = ((own_part[k, :, cols].astype(F32) + there) * 0.5).astype(BF)
                if turned:
                    out[level, cols, :] = mean.T
                else:
                    out[level, :, cols] = mean
                plan.work(0.6)
                yield from plan.need()

        return [first_part(), second_part()]

    def of(ref):
        return lambda cols: ref[:, :, :, :, cols].reshape(ROWS, QUARTER)

    def of_side(k):
        return lambda cols: side[:, :, :, k * SLOTS : (k + 1) * SLOTS, cols].reshape(ROWS, QUARTER)

    def both(name):
        return [((name, True), 2), ((name, False), 2)]

    def spread(f, name, after):
        return [
            path_gather(
                w,
                plan,
                lambda q, p=plane_of(mine): f.at[q, p],
                name,
                [((after, mine), 1)],
            )
            for mine in (True, False)
        ]

    main = [load_weights()]
    main += gather(w, plan, n1, "n1", [])
    main += [first(True), first(False)]
    main += reduce(w, plan, part1, red1, "red1", "part1")
    main += [middle()]
    main += gather(w, plan, n2, "n2", [("n2_own", 1)])
    main += [second(True), second(False)]
    main += reduce(w, plan, part2, red2, "red2", "part2")
    main += [back()]
    main += gather(w, plan, dh, "dh", [("dh_own", 1)])
    main += [third(True), third(False)]
    tail = [path_gather(w, plan, lambda q: r_dh.at[q], "r_dh", [("dh_own", 1)]), side_dh()]
    tail += gather(w, plan, dhq, "dhq", [("dhq_own", 1)])
    tail += spread(f_a1, "f_a1", "a1")
    low = [path_gather(w, plan, lambda q: r_dy.at[q], "r_dy", [])]
    low += [path_gather(w, plan, lambda q: r_n1.at[q], "r_n1", [])]
    low += [side_rows()]
    low += gather(w, plan, side, "side", [("side_rows", 1)])
    low += [pull(True), pull(False)]
    low += spread(f_u1, "f_u1", "part1")
    low += [path_gather(w, plan, lambda q: r_n2.at[q], "r_n2", [("n2_own", 1)]), side_n2()]
    low += spread(f_u2, "f_u2", "part2")
    low += spread(f_a2, "f_a2", "part2")
    low += gather(w, plan, n2q, "n2q", [("n2q_own", 1)])

    high_out = delta(
        d_out, 1, 0, f_u2, mate_high, of_side(0), of_side(2),
        both("side") + [(("part2", True), 1), (("part2", False), 1)], [("f_u2", 2)], False,
    )
    high_in = delta(
        d_in, 1, 1, f_a2, mate_high, of(n2), of(n2q),
        both("n2") + [(("part2", True), 1), (("part2", False), 1)], [("f_a2", 2)] + both("n2q"), True,
    )
    low_out = delta(
        d_out, 0, 2, f_u1, mate_low, of(dh), of(dhq),
        both("dh"), [("f_u1", 2)] + both("dhq"), False,
    )
    low_in = delta(
        d_in, 0, 3, f_a1, mate_low, of(n1), of_side(1),
        [(("a1", True), 1), (("a1", False), 1)], [("f_a1", 2)] + both("side"), True,
    )
    low += high_out + high_in
    tail += low_out + low_in
    plan.run([(0.0, t) for t in main] + [(0.5, t) for t in tail] + [(SIDE_LAG, t) for t in low])
    w.drain()


def step_call(tokens, routes, cotangent, gains, w_in, w_out, partners):
    anywhere = pl.BlockSpec(memory_space=pl.ANY)
    vmem = pl.BlockSpec(memory_space=pltpu.VMEM)

    def full(rows):
        return pltpu.VMEM((2, 4, 4, rows, WIDTH), BF)

    def by_path():
        return pltpu.VMEM((8, SLOTS, WIDTH), BF)

    def factor():
        return pltpu.VMEM((8, 2, PLANE, HIDDEN), BF)

    return pl.pallas_call(
        step_kernel,
        out_shape=[
            jax.ShapeDtypeStruct((2, WIDTH, HIDDEN), BF),
            jax.ShapeDtypeStruct((2, HIDDEN, WIDTH), BF),
        ],
        in_specs=[pl.BlockSpec(memory_space=pltpu.SMEM)] + [vmem] * 4 + [anywhere] * 2,
        out_specs=[vmem, vmem],
        scratch_shapes=[
            pltpu.VMEM((8, 2, 2, WIDTH), BF),
            pltpu.VMEM((8, 2, 2, WIDTH), BF),
            pltpu.VMEM((SLOTS, WIDTH), F32),
            pltpu.VMEM((SLOTS, WIDTH), F32),
            pltpu.VMEM((2, WIDTH, HIDDEN), BF),
            pltpu.VMEM((2, HIDDEN, WIDTH), BF),
            full(SLOTS),
            full(SLOTS),
            full(SLOTS),
            full(3 * SLOTS),
            full(SLOTS),
            full(SLOTS),
            by_path(),
            by_path(),
            by_path(),
            by_path(),
            factor(),
            factor(),
            factor(),
            factor(),
            pltpu.VMEM((2, PLANE, HIDDEN), F32),
            pltpu.VMEM((2, PLANE, HIDDEN), F32),
            pltpu.VMEM((2, PLANE, HIDDEN), F32),
            pltpu.VMEM((4, HIDDEN, WIDTH), BF),
            full(SLOTS),
            full(SLOTS),
        ]
        + reduce_scratch()
        + reduce_scratch()
        + [
            pltpu.SemaphoreType.DMA((2,)),
            pltpu.SemaphoreType.DMA((COPIES,)),
            pltpu.SemaphoreType.DMA((COPIES,)),
        ],
        compiler_params=pltpu.CompilerParams(
            collective_id=0, has_side_effects=True, vmem_limit_bytes=62 << 20
        ),
    )(partners, tokens, routes, cotangent, gains, w_in, w_out)


def body(tokens, routes, cotangent, gains, w_in, w_out, partners):
    d_in, d_out = step_call(tokens, routes, cotangent, gains, w_in, w_out, partners)
    return d_in[None], d_out[None]


def solution(mesh):
    in_specs = (
        P(("path", "shard"), None),
        P(("path", "shard"), None),
        P(("path", "shard"), None),
        P("path", None, None),
        P("path", None, None, "shard"),
        P("path", None, "shard", None),
        P(),
    )
    out_specs = (P("path", None, None, "shard"), P("path", None, "shard", None))
    return jax.shard_map(body, mesh=mesh, in_specs=in_specs, out_specs=out_specs, check_vma=False)
```

```python
import jax
import jax.numpy as jnp
from jax import lax
from jax.experimental import pallas as pl
from jax.experimental.pallas import tpu as pltpu
from jax.sharding import PartitionSpec as P

SLOTS = 16
MESH = pl.DeviceIdType.MESH
BF = jnp.bfloat16
F32 = jnp.float32
WIDTH = 2048
HALF = 1024
QUARTER = 512
HIDDEN = 256
ROWS = 512
PLANE = 256
COPIES = 480
RATE = 90000.0
DELAY = 2.5
DIRECT_REDUCE = False
STRAIGHT = {'n2': (True, False), 'n2q': (True, False), 'dh': (False, False), 'n1': (True, False), 'dy': (False, False), 'side': (False, False), 'dhq': (True, False)}
LAGS = {'dy': (29.6, 4.3), 'r_dy': (10.5, 9.6), 'r_n1': (0.1, 5.8), 'side': (23.6, 9.6), 'f_u1': (6.4, 4.3), 'r_n2': (5.9, 3.2), 'f_u2': (18.0, 3.4), 'f_a2': (2.0, 8.3), 'n2q': (3.0, 3.6), 'high': (2.8, 1.6), 'own': (9.0, 0.5), 'r_dh': (2.2, 0.1), 'dhq': (0.0, 6.8), 'f_a1': (1.2, 7.7), 'pull': (2.1, 7.0), 'second': (1.2, 3.2), 'first': (1.7, 0.0), 'end': (4.5, 5.0), 'n1': (0.0, 6.1), 'dh': (0.0, 1.1), 'red1': (2.0, 2.8), 'red2': (0.0, 0.0), 'n2': (0.0, 4.2), 'third': (4.0, 0.1)}


class Wires:
    def __init__(self, plan, send, recv):
        self.plan, self.send, self.recv, self.made = plan, send, recv, []
        path = lax.axis_index("path")
        self.path = path
        self.zl, self.core = path // 2, lax.rem(path, 2)
        self.z_two = lax.rem(self.zl + 2, 4)
        self.z_one = self.zl + 1 - 2 * lax.rem(self.zl, 2)
        shard = lax.axis_index("shard")
        self.zh = shard // 16
        self.x = lax.rem(shard // 4, 4)
        self.y = lax.rem(shard, 4)

    def shard(self, zh, x, y):
        return {"shard": zh * 16 + x * 4 + y}

    def xs(self, step):
        return lax.rem(self.x + step + 4, 4)

    def ys(self, step):
        return lax.rem(self.y + step + 4, 4)

    def pos(self, axis, step):
        return self.xs(step) if axis == "x" else self.ys(step)

    def beside(self, axis, step):
        if axis == "x":
            to = self.shard(self.zh, self.xs(step), self.y)
        else:
            to = self.shard(self.zh, self.x, self.ys(step))
        ways = {1: "+", -1: "-", 2: "+-"}[step]
        return to, [(axis + way, 2.0) for way in ways]

    def across(self):
        return self.shard(1 - self.zh, self.x, self.y), [("zm", 4.0), ("ze", 4.0), ("far", 0.0)]

    def level_with(self, z, links):
        return {"path": z * 2 + self.core}, links

    def sibling(self):
        return {"path": self.zl * 2 + 1 - self.core}, [("core", 0.4)]

    def peers(self):
        for dz in range(4):
            for dc in range(2):
                if dz or dc:
                    core = lax.rem(self.core + dc, 2)
                    yield lax.rem(self.zl + dz, 4) * 2 + core

    def push(self, src, dst, where):
        to, links = where
        k = len(self.made)
        copy = pltpu.make_async_remote_copy(
            src_ref=src,
            dst_ref=dst,
            send_sem=self.send.at[k],
            recv_sem=self.recv.at[k],
            device_id=to,
            device_id_type=MESH,
        )
        copy.start()
        size = 2
        for extent in src.shape:
            size *= extent
        self.made.append(copy)
        self.plan.sent(copy, size, links)
        return copy

    def drain(self):
        for copy in self.made:
            copy.wait_send()

    def greet(self, meanwhile):
        barrier = pltpu.get_barrier_semaphore()
        peers = [self.beside(axis, step)[0] for axis in "xy" for step in (1, -1, 2)]
        peers += [self.across()[0]]
        for to in self.peers():
            peers += [{"path": to}, {"path": to, **self.across()[0]}]
        for to in peers:
            pl.semaphore_signal(barrier, inc=1, device_id=to, device_id_type=MESH)
        meanwhile()
        pl.semaphore_wait(barrier, len(peers))


class Plan:
    def __init__(self):
        self.clock, self.free, self.due, self.marks = 0.0, {}, {}, {}
        self.used, self.stall = {}, 0.0

    def sent(self, copy, size, links):
        end = self.clock
        for name, load in links:
            if name == "far":
                end += 1.5
                continue
            start = max(self.clock, self.free.get(name, 0.0))
            self.free[name] = start + size * load / RATE
            self.used[name] = self.used.get(name, 0.0) + size * load / RATE
            end = max(end, self.free[name])
        self.due[id(copy)] = end + DELAY
        self.clock += 0.08

    def work(self, time):
        self.clock += time

    def mark(self, name):
        self.marks.setdefault(name, []).append(self.clock)

    def need(self, *names):
        yield "marks", names

    def ready(self, state):
        kind, items = state
        if kind == "copies":
            return max(self.due[id(copy)] for copy in items)
        times = [0.0]
        for name, count in items:
            have = self.marks.get(name, [])
            if len(have) < count:
                return None
            times.append(have[count - 1])
        return max(times)

    def run(self, tasks):
        tasks = [[{"marks": early, "copies": lag}, task, None] for early, lag, task in tasks]
        for entry in tasks:
            entry[2] = next(entry[1])
        while tasks:
            best = None
            for entry in tasks:
                time = self.ready(entry[2])
                if time is None:
                    continue
                time = max(time + entry[0][entry[2][0]], self.clock)
                if best is None or time < best[0] - 1e-6:
                    best = (time, entry)
            time, entry = best
            self.clock = max(self.clock, self.ready(entry[2]))
            try:
                entry[2] = next(entry[1])
            except StopIteration:
                tasks.remove(entry)


def ring_gather(w, axis, view, low, size):
    here, left, right = w.pos(axis, 0), w.pos(axis, -1), w.pos(axis, 1)
    to_right, to_left = w.beside(axis, 1), w.beside(axis, -1)
    half = size // 2
    first, last = view(here, low, half), view(here, low + half, half)
    right_first = w.push(first, first, to_right)
    left_first = w.push(last, last, to_left)
    right_rest = w.push(last, last, to_right)
    left_rest = w.push(first, first, to_left)
    yield "copies", [right_first]
    right_first.wait_recv()
    part = view(left, low, half)
    right_on = w.push(part, part, to_right)
    yield "copies", [left_first]
    left_first.wait_recv()
    part = view(right, low + half, half)
    left_on = w.push(part, part, to_left)
    ends = [right_rest, left_rest, right_on, left_on]
    yield "copies", ends
    for copy in ends:
        copy.wait_recv()


def ring_share(w, axis, view, low, size):
    own = view(w.pos(axis, 0), low, size)
    sent = [w.push(own, own, w.beside(axis, step)) for step in (1, -1, 2)]
    yield "copies", sent
    for copy in sent:
        copy.wait_recv()


def gather(w, plan, full, name, after):
    straight = STRAIGHT.get(name, (True, False))

    def half(mine, first, second, low):
        plane = w.zh if mine else 1 - w.zh
        yield from plan.need(*after)

        def line(i, start, size):
            cols = pl.ds(start, size)
            if first == "x":
                return full.at[plane, i, w.y, :, cols]
            return full.at[plane, w.x, i, :, cols]

        def sheet(i, start, size):
            cols = pl.ds(start, size)
            if second == "x":
                return full.at[plane, i, :, :, cols]
            return full.at[plane, :, i, :, cols]

        yield from (ring_share if straight[0] else ring_gather)(w, first, line, low, HALF)
        yield from (ring_share if straight[1] else ring_gather)(w, second, sheet, low, HALF)
        plan.mark((name, mine))

    return [
        half(True, "x", "y", 0),
        half(True, "y", "x", HALF),
        half(False, "x", "y", 0),
        half(False, "y", "x", HALF),
    ]


class Mates:
    def __init__(self, w, partners, level):
        def kept(path, other):
            mate = partners[level, path]
            z, core = mate // 2, lax.rem(mate, 2)
            far = 2 + core
            return jnp.where(z == w.zl, core, jnp.where(z == w.z_two, far, other))

        self.here = kept(w.path, 4)
        self.there = kept(w.z_one * 2 + w.core, 0)


def path_fetch(w, plan, view, load, keep, stage, mates, name, after):
    yield from plan.need(*after)
    own, far = view(w.core), view(2 + w.core)
    two = w.push(own, far, w.level_with(w.z_two, [("zm", 4.0), ("ze", 2.0)]))
    aside = w.push(own, own, w.sibling())
    yield "copies", [two]
    two.wait_recv()
    over = w.push(far, far, w.sibling())
    yield "copies", [aside, over]
    aside.wait_recv()
    over.wait_recv()
    out, late = stage
    out[...] = load(mates.there)
    last = w.push(out, late, w.level_with(w.z_one, [("ze", 2.0)]))
    yield "copies", [last]
    last.wait_recv()
    keep(late[...])
    plan.mark(name)


def ring_reduce(w, axis, view, low, bufs, out):
    from_left, from_right, in_r_lo, in_r_hi, in_l_lo, in_l_hi, tmp_r, tmp_l = bufs
    q = QUARTER
    here, left, right, far = (w.pos(axis, s) for s in (0, -1, 1, 2))
    to_right, to_left = w.beside(axis, 1), w.beside(axis, -1)
    a = w.push(view(far, low, q), from_left, to_right)
    b = w.push(view(far, low + q, q), from_right, to_left)
    c = w.push(view(right, low + q, q), in_r_hi, to_right)
    d = w.push(view(left, low, q), in_l_lo, to_left)
    yield "copies", [a]
    a.wait_recv()
    tmp_r[...] = (view(right, low, q)[...].astype(F32) + from_left[...].astype(F32)).astype(BF)
    w.plan.work(0.2)
    e = w.push(tmp_r, in_r_lo, to_right)
    yield "copies", [b]
    b.wait_recv()
    tmp_l[...] = (view(left, low + q, q)[...].astype(F32) + from_right[...].astype(F32)).astype(BF)
    w.plan.work(0.2)
    f = w.push(tmp_l, in_l_hi, to_left)
    yield "copies", [c, d, e, f]
    for copy in (c, d, e, f):
        copy.wait_recv()
    out(0, view(here, low, q)[...].astype(F32) + in_r_lo[...].astype(F32) + in_l_lo[...].astype(F32))
    out(
        1,
        view(here, low + q, q)[...].astype(F32)
        + in_r_hi[...].astype(F32)
        + in_l_hi[...].astype(F32),
    )
    w.plan.work(0.4)


def ring_total(w, axis, view, bufs, out):
    sent = [
        w.push(view(w.pos(axis, step)), buf, w.beside(axis, step))
        for step, buf in zip((1, -1, 2), bufs)
    ]
    yield "copies", sent
    for copy in sent:
        copy.wait_recv()
    value = view(w.pos(axis, 0))[...].astype(F32)
    for buf in bufs:
        value = value + buf[...].astype(F32)
    out(value)
    w.plan.work(0.2)


def reduce(w, plan, part, scratch, name, after):
    big, small, mid, box, near, total = scratch
    over = {}

    def half(k, mine, first, second, low):
        plane = w.zh if mine else 1 - w.zh
        yield from plan.need(((after, mine), 1))

        def sheet(i, start, size):
            cols = pl.ds(start, size)
            if first == "x":
                return part.at[plane, i, :, :, cols]
            return part.at[plane, :, i, :, cols]

        def keep(which, value):
            mid[k, :, :, pl.ds(which * QUARTER, QUARTER)] = value.astype(BF)

        def keep_all(value):
            mid[k] = value.astype(BF)

        def line(i):
            return mid.at[k, i]

        def last(value):
            cols = pl.ds(low, HALF)
            box[plane, :, cols] = value.astype(BF)

        if DIRECT_REDUCE:
            bufs = [big.at[k, n] for n in range(3)]
            yield from ring_total(w, first, lambda i: sheet(i, low, HALF), bufs, keep_all)
        else:
            yield from ring_reduce(w, first, sheet, low, [big.at[k, n] for n in range(8)], keep)
        yield from ring_total(w, second, line, [small.at[k, n] for n in range(3)], last)
        cols = pl.ds(low, HALF)
        over[k] = w.push(box.at[plane, :, cols], near.at[plane, :, cols], w.across())
        plan.mark(name + "_part")

    def finish():
        yield from plan.need((name + "_part", 4))
        yield "copies", list(over.values())
        for copy in over.values():
            copy.wait_recv()
        total[...] = box[...].astype(F32) + near[...].astype(F32)
        plan.mark(name)

    return [
        half(0, False, "x", "y", 0),
        half(1, False, "y", "x", HALF),
        half(2, True, "x", "y", 0),
        half(3, True, "y", "x", HALF),
        finish(),
    ]


def reduce_scratch():
    return [
        pltpu.VMEM((4, 3, 4, SLOTS, HALF) if DIRECT_REDUCE else (4, 8, 4, SLOTS, QUARTER), BF),
        pltpu.VMEM((4, 3, SLOTS, HALF), BF),
        pltpu.VMEM((4, 4, SLOTS, HALF), BF),
        pltpu.VMEM((2, SLOTS, WIDTH), BF),
        pltpu.VMEM((2, SLOTS, WIDTH), BF),
        pltpu.VMEM((2, SLOTS, WIDTH), F32),
    ]


def norm_rows(v, gain):
    return v * lax.rsqrt(jnp.mean(v * v, axis=-1, keepdims=True) + 1e-05) * gain.astype(F32)


def norm_pull(v, gain, grad):
    turn = lax.rsqrt(jnp.mean(v * v, axis=-1, keepdims=True) + 1e-05)
    scaled = grad * gain.astype(F32)
    along = jnp.mean(scaled * v, axis=-1, keepdims=True)
    return turn * scaled - v * (turn * turn * turn * along)


def gelu_both(a):
    c = 0.7978845608028654
    square = a * a
    t = jnp.tanh(c * (a + 0.044715 * a * square))
    value = 0.5 * a * (1.0 + t)
    slope = 0.5 * (1.0 + t) + 0.5 * a * (1.0 - t * t) * (c * (1.0 + 3.0 * 0.044715 * square))
    return value, slope


def dot(a, b):
    return jnp.dot(a, b, preferred_element_type=F32)


def dot_t(a, b):
    return lax.dot_general(a, b, (((1,), (1,)), ((), ())), preferred_element_type=F32)


def step_kernel(
    partners,
    tokens,
    routes,
    cotangent,
    gains,
    w_in,
    w_out,
    d_in,
    d_out,
    packed,
    got,
    x_own,
    dy_own,
    wi,
    wo,
    n1,
    n2,
    dh,
    dy,
    side,
    n2q,
    dhq,
    r_n1,
    r_dy,
    r_n2,
    r_dh,
    row_stage,
    row_late,
    f_u1_near,
    f_u1_far,
    f_a1_near,
    f_a1_far,
    f_u2_near,
    f_u2_far,
    f_a2_near,
    f_a2_far,
    stage,
    late,
    slope1,
    slope2,
    pull2,
    own_part,
    part1,
    part2,
    *rest,
):
    red1, red2 = rest[0:6], rest[6:12]
    load, send, recv = rest[12:]
    plan = Plan()
    w = Wires(plan, send, recv)
    me = w.path
    f_u1, f_a1 = (f_u1_near, f_u1_far), (f_a1_near, f_a1_far)
    f_u2, f_a2 = (f_u2_near, f_u2_far), (f_a2_near, f_a2_far)
    mate_low, mate_high = Mates(w, partners, 0), Mates(w, partners, 1)
    scale = 1.0 / jnp.sqrt(jnp.float32(ROWS))
    loads = [
        pltpu.make_async_copy(w_in.at[0], wi, load.at[0]),
        pltpu.make_async_copy(w_out.at[0], wo, load.at[1]),
    ]
    for copy in loads:
        copy.start()

    def pack():
        count = tokens.shape[0]
        route = routes[...]
        named = (route == lax.broadcasted_iota(jnp.int32, (count, 128), 1)).astype(BF)
        same = dot_t(named, named)
        before = lax.broadcasted_iota(jnp.int32, same.shape, 1) < lax.broadcasted_iota(
            jnp.int32, same.shape, 0
        )
        rank = jnp.sum(jnp.where(before, same, 0.0), axis=1, keepdims=True)
        place = route.astype(F32) * 2.0 + rank
        slot = lax.broadcasted_iota(jnp.int32, (count, SLOTS), 1).astype(F32)
        select = (place == slot).astype(BF)
        for k, rows in enumerate((tokens, cotangent)):
            sorted_rows = lax.dot_general(
                select, rows[...], (((0,), (0,)), ((), ())), preferred_element_type=F32
            )
            for p in range(8):
                packed[p, k] = sorted_rows[2 * p : 2 * p + 2].astype(BF)

    w.greet(pack)
    hops, landing = [], got.at[w.zh, me]
    for to in w.peers():
        for where in ({"path": to}, {"path": to, **w.across()[0]}):
            hops.append(w.push(packed.at[to], landing, (where, [("zm", 2.0), ("ze", 2.0)])))
    hops.append(w.push(packed.at[me], landing, w.across()))
    got[w.zh, me] = packed[me]
    for copy in hops:
        copy.wait_recv()
    for z in range(2):
        for p in range(8):
            x_own[z, 2 * p : 2 * p + 2, :] = got[z, p, 0].astype(F32)
            dy_own[z, 2 * p : 2 * p + 2, :] = got[z, p, 1].astype(F32)

    def spread_rows(full, rows, start=0):
        for z in range(2):
            full[z, w.x, w.y, start : start + SLOTS] = rows[z]

    rows_n1 = norm_rows(x_own[...], gains[0, 0:1, :]).astype(BF)
    spread_rows(n1, rows_n1)
    r_n1[w.core] = rows_n1
    rows_dy = dy_own[...].astype(BF)
    spread_rows(dy, rows_dy)
    r_dy[w.core] = rows_dy

    def index(mine):
        return 0 if mine else 1

    def plane_of(mine):
        return w.zh if mine else 1 - w.zh

    def load_weights():
        yield from plan.need()
        for copy in loads:
            copy.wait()
        plan.mark("weights")

    def side_rows():
        yield from plan.need(("r_n1", 1), ("r_dy", 1))
        spread_rows(side, r_n1[mate_low.here])
        spread_rows(side, r_dy[mate_high.here], SLOTS)
        plan.mark("side_rows")

    def first(mine):
        p = plane_of(mine)
        yield from plan.need((("n1", mine), 2), ("weights", 1))
        a = dot(n1[p].reshape(PLANE, WIDTH), wi[0])
        value, slope = gelu_both(a)
        u = value.astype(BF)
        slope1[p] = slope
        f_u1[index(mine)][w.core] = u
        for c in range(0, WIDTH, QUARTER):
            y = dot(u, wo[0, :, c : c + QUARTER]).astype(BF)
            part1[p, :, :, :, c : c + QUARTER] = y.reshape(4, 4, SLOTS, QUARTER)
        plan.work(2.0)
        plan.mark(("part1", mine))
        plan.mark("u1")

    def middle():
        yield from plan.need(("red1", 1))
        h = (x_own[...] + red1[5][...]).astype(BF).astype(F32)
        rows = norm_rows(h, gains[0, 1:2, :]).astype(BF)
        spread_rows(n2, rows)
        r_n2[w.core] = rows
        plan.work(0.6)
        plan.mark("n2_own")

    def pull(mine):
        p = plane_of(mine)
        yield from plan.need((("dy", mine), 2), ("weights", 1))
        pull2[p] = dot_t(dy[p].reshape(PLANE, WIDTH), wo[1])
        plan.work(0.8)
        plan.mark(("pull2", mine))

    def second(mine):
        p = plane_of(mine)
        yield from plan.need((("n2", mine), 2), (("pull2", mine), 1))
        a = dot(n2[p].reshape(PLANE, WIDTH), wi[1])
        value, slope = gelu_both(a)
        f_u2[index(mine)][w.core] = value.astype(BF)
        da = (pull2[p] * slope).astype(BF)
        f_a2[index(mine)][w.core] = da
        for c in range(0, WIDTH, QUARTER):
            y = dot_t(da, wi[1, c : c + QUARTER, :]).astype(BF)
            part2[p, :, :, :, c : c + QUARTER] = y.reshape(4, 4, SLOTS, QUARTER)
        plan.work(2.0)
        plan.mark(("part2", mine))
        plan.mark("u2")

    def side_n2():
        yield from plan.need(("r_n2", 1))
        spread_rows(n2q, r_n2[mate_high.here])
        plan.mark("n2q_own")

    def back():
        yield from plan.need(("red2", 1))
        h = (x_own[...] + red1[5][...]).astype(BF).astype(F32)
        grad = norm_pull(h, gains[0, 1:2, :], red2[5][...])
        rows = (dy_own[...] + grad).astype(BF)
        spread_rows(dh, rows)
        r_dh[w.core] = rows
        plan.work(0.8)
        plan.mark("dh_own")

    def side_dh():
        yield from plan.need(("r_dh", 1))
        spread_rows(dhq, r_dh[mate_low.here])
        plan.mark("dhq_own")

    def third(mine):
        p = plane_of(mine)
        yield from plan.need((("dh", mine), 2))
        du = dot_t(dh[p].reshape(PLANE, WIDTH), wo[0])
        f_a1[index(mine)][w.core] = (du * slope1[p]).astype(BF)
        plan.work(0.8)
        plan.mark(("a1", mine))

    def in_order(factor, k):
        near, far = factor[0][k], factor[1][k]
        swap = w.zh == 1
        top, bottom = jnp.where(swap, far, near), jnp.where(swap, near, far)
        return jnp.concatenate([top, bottom], axis=0).T

    def delta(out, level, k, own, mate, own_rows, mate_rows, own_needs, mate_needs, turned):
        def product(factor, rows, cols):
            return (-dot(factor, rows(cols)) * scale).astype(BF)

        def first_part():
            yield from plan.need(*own_needs)
            factor = in_order(own, w.core)
            for c in range(0, WIDTH, QUARTER):
                cols = slice(c, c + QUARTER)
                own_part[k, :, cols] = product(factor, own_rows, cols)
                plan.work(0.15)
                yield from plan.need()
            plan.mark(("delta", k))

        def second_part():
            yield from plan.need((("delta", k), 1), *mate_needs)
            factor = in_order(own, mate.here)
            for c in range(0, WIDTH, QUARTER):
                cols = slice(c, c + QUARTER)
                there = product(factor, mate_rows, cols).astype(F32)
                mean = ((own_part[k, :, cols].astype(F32) + there) * 0.5).astype(BF)
                if turned:
                    out[level, cols, :] = mean.T
                else:
                    out[level, :, cols] = mean
                plan.work(0.22)
                yield from plan.need()

        return [first_part(), second_part()]

    def of(ref):
        return lambda cols: ref[:, :, :, :, cols].reshape(ROWS, QUARTER)

    def of_side(k):
        return lambda cols: side[:, :, :, k * SLOTS : (k + 1) * SLOTS, cols].reshape(ROWS, QUARTER)

    def both(name):
        return [((name, True), 2), ((name, False), 2)]

    def spread(f, number, mates, name, after):
        for mine in (True, False):
            i = index(mine)

            def keep(value, i=i):
                f[i][4] = value

            yield path_fetch(
                w,
                plan,
                lambda k, i=i: f[i].at[k],
                lambda k, i=i: f[i][k],
                keep,
                (stage.at[number, i], late.at[number, i]),
                mates,
                name,
                [((after, mine), 1)],
            )

    def rows_over(ref, number, mates, name, after):
        def keep(value):
            ref[4] = value

        return path_fetch(
            w,
            plan,
            lambda k: ref.at[k],
            lambda k: ref[k],
            keep,
            (row_stage.at[number], row_late.at[number]),
            mates,
            name,
            after,
        )

    def parts(name):
        return [((name, True), 1), ((name, False), 1)]

    high_out = delta(
        d_out, 1, 0, f_u2, mate_high, of(dy), of_side(1),
        both("dy") + parts("part2"), [("f_u2", 2)] + both("side"), False,
    )
    high_in = delta(
        d_in, 1, 1, f_a2, mate_high, of(n2), of(n2q),
        both("n2") + parts("part2"), [("f_a2", 2)] + both("n2q"), True,
    )
    low_out = delta(
        d_out, 0, 2, f_u1, mate_low, of(dh), of(dhq),
        both("dh"), [("f_u1", 2)] + both("dhq"), False,
    )
    low_in = delta(
        d_in, 0, 3, f_a1, mate_low, of(n1), of_side(0),
        parts("a1"), [("f_a1", 2)] + both("side"), True,
    )
    groups = [
        ("load", [load_weights()]),
        ("n1", gather(w, plan, n1, "n1", [])),
        ("first", [first(True), first(False)]),
        ("red1", reduce(w, plan, part1, red1, "red1", "part1")),
        ("mid", [middle()]),
        ("n2", gather(w, plan, n2, "n2", [("n2_own", 1)])),
        ("second", [second(True), second(False)]),
        ("red2", reduce(w, plan, part2, red2, "red2", "part2")),
        ("back", [back()]),
        ("dh", gather(w, plan, dh, "dh", [("dh_own", 1)])),
        ("third", [third(True), third(False)]),
        ("r_dh", [rows_over(r_dh, 3, mate_low, "r_dh", [("dh_own", 1)]), side_dh()]),
        ("dhq", gather(w, plan, dhq, "dhq", [("dhq_own", 1)])),
        ("f_a1", spread(f_a1, 1, mate_low, "f_a1", "a1")),
        ("own", [low_out[0], low_in[0]]),
        ("end", [low_out[1], low_in[1]]),
        ("dy", gather(w, plan, dy, "dy", [])),
        ("pull", [pull(True), pull(False)]),
        ("r_dy", [rows_over(r_dy, 1, mate_high, "r_dy", [])]),
        ("r_n1", [rows_over(r_n1, 0, mate_low, "r_n1", []), side_rows()]),
        ("side", gather(w, plan, side, "side", [("side_rows", 1)])),
        ("f_u1", spread(f_u1, 0, mate_low, "f_u1", "part1")),
        ("r_n2", [rows_over(r_n2, 2, mate_high, "r_n2", [("n2_own", 1)]), side_n2()]),
        ("f_u2", spread(f_u2, 2, mate_high, "f_u2", "part2")),
        ("f_a2", spread(f_a2, 3, mate_high, "f_a2", "part2")),
        ("n2q", gather(w, plan, n2q, "n2q", [("n2q_own", 1)])),
        ("high", high_out + high_in),
    ]
    plan.run([LAGS.get(name, (0.0, 0.0)) + (t,) for name, tasks in groups for t in tasks])
    w.drain()


def step_call(tokens, routes, cotangent, gains, w_in, w_out, partners):
    anywhere = pl.BlockSpec(memory_space=pl.ANY)
    vmem = pl.BlockSpec(memory_space=pltpu.VMEM)

    def full(rows):
        return pltpu.VMEM((2, 4, 4, rows, WIDTH), BF)

    def by_path():
        return pltpu.VMEM((5, 2, SLOTS, WIDTH), BF)

    def factor():
        return pltpu.VMEM((5, PLANE, HIDDEN), BF)

    return pl.pallas_call(
        step_kernel,
        out_shape=[
            jax.ShapeDtypeStruct((2, WIDTH, HIDDEN), BF),
            jax.ShapeDtypeStruct((2, HIDDEN, WIDTH), BF),
        ],
        in_specs=[pl.BlockSpec(memory_space=pltpu.SMEM)] + [vmem] * 4 + [anywhere] * 2,
        out_specs=[vmem, vmem],
        scratch_shapes=[
            pltpu.VMEM((8, 2, 2, WIDTH), BF),
            pltpu.VMEM((2, 8, 2, 2, WIDTH), BF),
            pltpu.VMEM((2, SLOTS, WIDTH), F32),
            pltpu.VMEM((2, SLOTS, WIDTH), F32),
            pltpu.VMEM((2, WIDTH, HIDDEN), BF),
            pltpu.VMEM((2, HIDDEN, WIDTH), BF),
            full(SLOTS),
            full(SLOTS),
            full(SLOTS),
            full(SLOTS),
            full(2 * SLOTS),
            full(SLOTS),
            full(SLOTS),
            by_path(),
            by_path(),
            by_path(),
            by_path(),
            pltpu.VMEM((4, 2, SLOTS, WIDTH), BF),
            pltpu.VMEM((4, 2, SLOTS, WIDTH), BF),
            factor(),
            factor(),
            factor(),
            factor(),
            factor(),
            factor(),
            factor(),
            factor(),
            pltpu.VMEM((4, 2, PLANE, HIDDEN), BF),
            pltpu.VMEM((4, 2, PLANE, HIDDEN), BF),
            pltpu.VMEM((2, PLANE, HIDDEN), F32),
            pltpu.VMEM((2, PLANE, HIDDEN), F32),
            pltpu.VMEM((2, PLANE, HIDDEN), F32),
            pltpu.VMEM((4, HIDDEN, WIDTH), BF),
            full(SLOTS),
            full(SLOTS),
        ]
        + reduce_scratch()
        + reduce_scratch()
        + [
            pltpu.SemaphoreType.DMA((2,)),
            pltpu.SemaphoreType.DMA((COPIES,)),
            pltpu.SemaphoreType.DMA((COPIES,)),
        ],
        compiler_params=pltpu.CompilerParams(
            collective_id=0, has_side_effects=True, vmem_limit_bytes=62 << 20
        ),
    )(partners, tokens, routes, cotangent, gains, w_in, w_out)


def body(tokens, routes, cotangent, gains, w_in, w_out, partners):
    d_in, d_out = step_call(tokens, routes, cotangent, gains, w_in, w_out, partners)
    return d_in[None], d_out[None]


def solution(mesh):
    in_specs = (
        P(("path", "shard"), None),
        P(("path", "shard"), None),
        P(("path", "shard"), None),
        P("path", None, None),
        P("path", None, None, "shard"),
        P("path", None, "shard", None),
        P(),
    )
    out_specs = (P("path", None, None, "shard"), P("path", None, "shard", None))
    return jax.shard_map(body, mesh=mesh, in_specs=in_specs, out_specs=out_specs, check_vma=False)
```

```python
import jax
import jax.numpy as jnp
from jax import lax
from jax.experimental import pallas as pl
from jax.experimental.pallas import tpu as pltpu
from jax.sharding import PartitionSpec as P

SLOTS = 16
MESH = pl.DeviceIdType.MESH
BF = jnp.bfloat16
F32 = jnp.float32
WIDTH = 2048
HALF = 1024
QUARTER = 512
HIDDEN = 256
ROWS = 512
PLANE = 256
COPIES = 480
RATE = 82000.0
DELAY = 2.5
DIRECT_REDUCE = False
STRAIGHT = {'n2': (True, False), 'n2q': (True, False), 'dh': (False, False), 'n1': (True, False), 'dy': (False, False), 'side': (False, False), 'dhq': (True, False)}
LAGS = {'dy': (29.6, 4.3), 'r_dy': (10.5, 9.6), 'r_n1': (0.1, 5.8), 'side': (23.6, 9.6), 'f_u1': (6.4, 4.3), 'r_n2': (5.9, 3.2), 'f_u2': (18.0, 3.4), 'f_a2': (2.0, 8.3), 'n2q': (3.0, 3.6), 'high': (2.8, 1.6), 'own': (9.0, 0.5), 'r_dh': (2.2, 0.1), 'dhq': (0.0, 6.8), 'f_a1': (1.2, 7.7), 'pull': (2.1, 7.0), 'second': (1.2, 3.2), 'first': (1.7, 0.0), 'end': (4.5, 5.0), 'n1': (0.0, 6.1), 'dh': (0.0, 1.1), 'red1': (2.0, 2.8), 'red2': (0.0, 0.0), 'n2': (0.0, 4.2), 'third': (4.0, 0.1)}


class Wires:
    def __init__(self, plan, send, recv):
        self.plan, self.send, self.recv, self.made = plan, send, recv, []
        path = lax.axis_index("path")
        self.path = path
        self.zl, self.core = path // 2, lax.rem(path, 2)
        self.z_two = lax.rem(self.zl + 2, 4)
        self.z_one = self.zl + 1 - 2 * lax.rem(self.zl, 2)
        shard = lax.axis_index("shard")
        self.zh = shard // 16
        self.x = lax.rem(shard // 4, 4)
        self.y = lax.rem(shard, 4)

    def shard(self, zh, x, y):
        return {"shard": zh * 16 + x * 4 + y}

    def xs(self, step):
        return lax.rem(self.x + step + 4, 4)

    def ys(self, step):
        return lax.rem(self.y + step + 4, 4)

    def pos(self, axis, step):
        return self.xs(step) if axis == "x" else self.ys(step)

    def beside(self, axis, step):
        if axis == "x":
            to = self.shard(self.zh, self.xs(step), self.y)
        else:
            to = self.shard(self.zh, self.x, self.ys(step))
        ways = {1: "+", -1: "-", 2: "+-"}[step]
        return to, [(axis + way, 2.0) for way in ways]

    def across(self):
        return self.shard(1 - self.zh, self.x, self.y), [("zm", 4.0), ("ze", 4.0), ("far", 0.0)]

    def level_with(self, z, links):
        return {"path": z * 2 + self.core}, links

    def sibling(self):
        return {"path": self.zl * 2 + 1 - self.core}, [("core", 0.4)]

    def peers(self):
        for dz in range(4):
            for dc in range(2):
                if dz or dc:
                    core = lax.rem(self.core + dc, 2)
                    yield lax.rem(self.zl + dz, 4) * 2 + core

    def push(self, src, dst, where):
        to, links = where
        k = len(self.made)
        copy = pltpu.make_async_remote_copy(
            src_ref=src,
            dst_ref=dst,
            send_sem=self.send.at[k],
            recv_sem=self.recv.at[k],
            device_id=to,
            device_id_type=MESH,
        )
        copy.start()
        size = 2
        for extent in src.shape:
            size *= extent
        self.made.append(copy)
        self.plan.sent(copy, size, links)
        return copy

    def drain(self):
        for copy in self.made:
            copy.wait_send()

    def greet(self, meanwhile):
        barrier = pltpu.get_barrier_semaphore()
        peers = [self.beside(axis, step)[0] for axis in "xy" for step in (1, -1, 2)]
        peers += [self.across()[0]]
        for to in self.peers():
            peers += [{"path": to}, {"path": to, **self.across()[0]}]
        for to in peers:
            pl.semaphore_signal(barrier, inc=1, device_id=to, device_id_type=MESH)
        meanwhile()
        pl.semaphore_wait(barrier, len(peers))


class Plan:
    def __init__(self):
        self.clock, self.free, self.due, self.marks = 0.0, {}, {}, {}
        self.used, self.stall = {}, 0.0

    def sent(self, copy, size, links):
        end = self.clock
        for name, load in links:
            if name == "far":
                end += 1.5
                continue
            start = max(self.clock, self.free.get(name, 0.0))
            self.free[name] = start + size * load / RATE
            self.used[name] = self.used.get(name, 0.0) + size * load / RATE
            end = max(end, self.free[name])
        self.due[id(copy)] = end + DELAY
        self.clock += 0.08

    def work(self, time):
        self.clock += time

    def mark(self, name):
        self.marks.setdefault(name, []).append(self.clock)

    def need(self, *names):
        yield "marks", names

    def ready(self, state):
        kind, items = state
        if kind == "copies":
            return max(self.due[id(copy)] for copy in items)
        times = [0.0]
        for name, count in items:
            have = self.marks.get(name, [])
            if len(have) < count:
                return None
            times.append(have[count - 1])
        return max(times)

    def run(self, tasks):
        tasks = [[{"marks": early, "copies": lag}, task, None] for early, lag, task in tasks]
        for entry in tasks:
            entry[2] = next(entry[1])
        while tasks:
            best = None
            for entry in tasks:
                time = self.ready(entry[2])
                if time is None:
                    continue
                time = max(time + entry[0][entry[2][0]], self.clock)
                if best is None or time < best[0] - 1e-6:
                    best = (time, entry)
            time, entry = best
            self.clock = max(self.clock, self.ready(entry[2]))
            try:
                entry[2] = next(entry[1])
            except StopIteration:
                tasks.remove(entry)


def ring_gather(w, axis, view, low, size):
    here, left, right = w.pos(axis, 0), w.pos(axis, -1), w.pos(axis, 1)
    to_right, to_left = w.beside(axis, 1), w.beside(axis, -1)
    half = size // 2
    first, last = view(here, low, half), view(here, low + half, half)
    right_first = w.push(first, first, to_right)
    left_first = w.push(last, last, to_left)
    right_rest = w.push(last, last, to_right)
    left_rest = w.push(first, first, to_left)
    yield "copies", [right_first]
    right_first.wait_recv()
    part = view(left, low, half)
    right_on = w.push(part, part, to_right)
    yield "copies", [left_first]
    left_first.wait_recv()
    part = view(right, low + half, half)
    left_on = w.push(part, part, to_left)
    ends = [right_rest, left_rest, right_on, left_on]
    yield "copies", ends
    for copy in ends:
        copy.wait_recv()


def ring_share(w, axis, view, low, size):
    own = view(w.pos(axis, 0), low, size)
    sent = [w.push(own, own, w.beside(axis, step)) for step in (1, -1, 2)]
    yield "copies", sent
    for copy in sent:
        copy.wait_recv()


def gather(w, plan, full, name, after):
    straight = STRAIGHT.get(name, (True, False))

    def half(mine, first, second, low):
        plane = w.zh if mine else 1 - w.zh
        yield from plan.need(*after)

        def line(i, start, size):
            cols = pl.ds(start, size)
            if first == "x":
                return full.at[plane, i, w.y, :, cols]
            return full.at[plane, w.x, i, :, cols]

        def sheet(i, start, size):
            cols = pl.ds(start, size)
            if second == "x":
                return full.at[plane, i, :, :, cols]
            return full.at[plane, :, i, :, cols]

        yield from (ring_share if straight[0] else ring_gather)(w, first, line, low, HALF)
        yield from (ring_share if straight[1] else ring_gather)(w, second, sheet, low, HALF)
        plan.mark((name, mine))

    return [
        half(True, "x", "y", 0),
        half(True, "y", "x", HALF),
        half(False, "x", "y", 0),
        half(False, "y", "x", HALF),
    ]


class Mates:
    def __init__(self, w, partners, level):
        def kept(path, other):
            mate = partners[level, path]
            z, core = mate // 2, lax.rem(mate, 2)
            far = 2 + core
            return jnp.where(z == w.zl, core, jnp.where(z == w.z_two, far, other))

        self.here = kept(w.path, 4)
        self.there = kept(w.z_one * 2 + w.core, 0)


def path_fetch(w, plan, view, load, keep, stage, mates, name, after):
    yield from plan.need(*after)
    own, far = view(w.core), view(2 + w.core)
    two = w.push(own, far, w.level_with(w.z_two, [("zm", 4.0), ("ze", 2.0)]))
    aside = w.push(own, own, w.sibling())
    yield "copies", [two]
    two.wait_recv()
    over = w.push(far, far, w.sibling())
    yield "copies", [aside, over]
    aside.wait_recv()
    over.wait_recv()
    out, late = stage
    out[...] = load(mates.there)
    last = w.push(out, late, w.level_with(w.z_one, [("ze", 2.0)]))
    yield "copies", [last]
    last.wait_recv()
    keep(late[...])
    plan.mark(name)


def ring_reduce(w, axis, view, low, bufs, out):
    from_left, from_right, in_r_lo, in_r_hi, in_l_lo, in_l_hi, tmp_r, tmp_l = bufs
    q = QUARTER
    here, left, right, far = (w.pos(axis, s) for s in (0, -1, 1, 2))
    to_right, to_left = w.beside(axis, 1), w.beside(axis, -1)
    a = w.push(view(far, low, q), from_left, to_right)
    b = w.push(view(far, low + q, q), from_right, to_left)
    c = w.push(view(right, low + q, q), in_r_hi, to_right)
    d = w.push(view(left, low, q), in_l_lo, to_left)
    yield "copies", [a]
    a.wait_recv()
    tmp_r[...] = (view(right, low, q)[...].astype(F32) + from_left[...].astype(F32)).astype(BF)
    w.plan.work(0.2)
    e = w.push(tmp_r, in_r_lo, to_right)
    yield "copies", [b]
    b.wait_recv()
    tmp_l[...] = (view(left, low + q, q)[...].astype(F32) + from_right[...].astype(F32)).astype(BF)
    w.plan.work(0.2)
    f = w.push(tmp_l, in_l_hi, to_left)
    yield "copies", [c, d, e, f]
    for copy in (c, d, e, f):
        copy.wait_recv()
    out(0, view(here, low, q)[...].astype(F32) + in_r_lo[...].astype(F32) + in_l_lo[...].astype(F32))
    out(
        1,
        view(here, low + q, q)[...].astype(F32)
        + in_r_hi[...].astype(F32)
        + in_l_hi[...].astype(F32),
    )
    w.plan.work(0.4)


def ring_total(w, axis, view, bufs, out):
    sent = [
        w.push(view(w.pos(axis, step)), buf, w.beside(axis, step))
        for step, buf in zip((1, -1, 2), bufs)
    ]
    yield "copies", sent
    for copy in sent:
        copy.wait_recv()
    value = view(w.pos(axis, 0))[...].astype(F32)
    for buf in bufs:
        value = value + buf[...].astype(F32)
    out(value)
    w.plan.work(0.2)


def reduce(w, plan, part, scratch, name, after):
    big, small, mid, box, near, total = scratch
    over = {}

    def half(k, mine, first, second, low):
        plane = w.zh if mine else 1 - w.zh
        yield from plan.need(((after, mine), 1))

        def sheet(i, start, size):
            cols = pl.ds(start, size)
            if first == "x":
                return part.at[plane, i, :, :, cols]
            return part.at[plane, :, i, :, cols]

        def keep(which, value):
            mid[k, :, :, pl.ds(which * QUARTER, QUARTER)] = value.astype(BF)

        def keep_all(value):
            mid[k] = value.astype(BF)

        def line(i):
            return mid.at[k, i]

        def last(value):
            cols = pl.ds(low, HALF)
            box[plane, :, cols] = value.astype(BF)

        if DIRECT_REDUCE:
            bufs = [big.at[k, n] for n in range(3)]
            yield from ring_total(w, first, lambda i: sheet(i, low, HALF), bufs, keep_all)
        else:
            yield from ring_reduce(w, first, sheet, low, [big.at[k, n] for n in range(8)], keep)
        yield from ring_total(w, second, line, [small.at[k, n] for n in range(3)], last)
        cols = pl.ds(low, HALF)
        over[k] = w.push(box.at[plane, :, cols], near.at[plane, :, cols], w.across())
        plan.mark(name + "_part")

    def finish():
        yield from plan.need((name + "_part", 4))
        yield "copies", list(over.values())
        for copy in over.values():
            copy.wait_recv()
        total[...] = box[...].astype(F32) + near[...].astype(F32)
        plan.mark(name)

    return [
        half(0, False, "x", "y", 0),
        half(1, False, "y", "x", HALF),
        half(2, True, "x", "y", 0),
        half(3, True, "y", "x", HALF),
        finish(),
    ]


def reduce_scratch():
    return [
        pltpu.VMEM((4, 3, 4, SLOTS, HALF) if DIRECT_REDUCE else (4, 8, 4, SLOTS, QUARTER), BF),
        pltpu.VMEM((4, 3, SLOTS, HALF), BF),
        pltpu.VMEM((4, 4, SLOTS, HALF), BF),
        pltpu.VMEM((2, SLOTS, WIDTH), BF),
        pltpu.VMEM((2, SLOTS, WIDTH), BF),
        pltpu.VMEM((2, SLOTS, WIDTH), F32),
    ]


def norm_rows(v, gain):
    return v * lax.rsqrt(jnp.mean(v * v, axis=-1, keepdims=True) + 1e-05) * gain.astype(F32)


def norm_pull(v, gain, grad):
    turn = lax.rsqrt(jnp.mean(v * v, axis=-1, keepdims=True) + 1e-05)
    scaled = grad * gain.astype(F32)
    along = jnp.mean(scaled * v, axis=-1, keepdims=True)
    return turn * scaled - v * (turn * turn * turn * along)


def gelu_both(a):
    c = 0.7978845608028654
    square = a * a
    t = jnp.tanh(c * (a + 0.044715 * a * square))
    value = 0.5 * a * (1.0 + t)
    slope = 0.5 * (1.0 + t) + 0.5 * a * (1.0 - t * t) * (c * (1.0 + 3.0 * 0.044715 * square))
    return value, slope


def dot(a, b):
    return jnp.dot(a, b, preferred_element_type=F32)


def dot_t(a, b):
    return lax.dot_general(a, b, (((1,), (1,)), ((), ())), preferred_element_type=F32)


def step_kernel(
    partners,
    tokens,
    routes,
    cotangent,
    gains,
    w_in,
    w_out,
    d_in,
    d_out,
    packed,
    got,
    x_own,
    dy_own,
    wi,
    wo,
    n1,
    n2,
    dh,
    dy,
    side,
    n2q,
    dhq,
    r_n1,
    r_dy,
    r_n2,
    r_dh,
    row_stage,
    row_late,
    f_u1_near,
    f_u1_far,
    f_a1_near,
    f_a1_far,
    f_u2_near,
    f_u2_far,
    f_a2_near,
    f_a2_far,
    stage,
    late,
    slope1,
    slope2,
    pull2,
    own_part,
    part1,
    part2,
    *rest,
):
    red1, red2 = rest[0:6], rest[6:12]
    load, send, recv = rest[12:]
    plan = Plan()
    w = Wires(plan, send, recv)
    me = w.path
    f_u1, f_a1 = (f_u1_near, f_u1_far), (f_a1_near, f_a1_far)
    f_u2, f_a2 = (f_u2_near, f_u2_far), (f_a2_near, f_a2_far)
    mate_low, mate_high = Mates(w, partners, 0), Mates(w, partners, 1)
    scale = 1.0 / jnp.sqrt(jnp.float32(ROWS))
    loads = [
        pltpu.make_async_copy(w_in.at[0], wi, load.at[0]),
        pltpu.make_async_copy(w_out.at[0], wo, load.at[1]),
    ]
    for copy in loads:
        copy.start()

    def pack():
        count = tokens.shape[0]
        route = routes[...]
        named = (route == lax.broadcasted_iota(jnp.int32, (count, 128), 1)).astype(BF)
        same = dot_t(named, named)
        before = lax.broadcasted_iota(jnp.int32, same.shape, 1) < lax.broadcasted_iota(
            jnp.int32, same.shape, 0
        )
        rank = jnp.sum(jnp.where(before, same, 0.0), axis=1, keepdims=True)
        place = route.astype(F32) * 2.0 + rank
        slot = lax.broadcasted_iota(jnp.int32, (count, SLOTS), 1).astype(F32)
        select = (place == slot).astype(BF)
        for k, rows in enumerate((tokens, cotangent)):
            sorted_rows = lax.dot_general(
                select, rows[...], (((0,), (0,)), ((), ())), preferred_element_type=F32
            )
            for p in range(8):
                packed[p, k] = sorted_rows[2 * p : 2 * p + 2].astype(BF)

    w.greet(pack)
    hops, landing = [], got.at[w.zh, me]
    for to in w.peers():
        for where in ({"path": to}, {"path": to, **w.across()[0]}):
            hops.append(w.push(packed.at[to], landing, (where, [("zm", 2.0), ("ze", 2.0)])))
    hops.append(w.push(packed.at[me], landing, w.across()))
    got[w.zh, me] = packed[me]
    for copy in hops:
        copy.wait_recv()
    for z in range(2):
        for p in range(8):
            x_own[z, 2 * p : 2 * p + 2, :] = got[z, p, 0].astype(F32)
            dy_own[z, 2 * p : 2 * p + 2, :] = got[z, p, 1].astype(F32)

    def spread_rows(full, rows, start=0):
        for z in range(2):
            full[z, w.x, w.y, start : start + SLOTS] = rows[z]

    rows_n1 = norm_rows(x_own[...], gains[0, 0:1, :]).astype(BF)
    spread_rows(n1, rows_n1)
    r_n1[w.core] = rows_n1
    rows_dy = dy_own[...].astype(BF)
    spread_rows(dy, rows_dy)
    r_dy[w.core] = rows_dy

    def index(mine):
        return 0 if mine else 1

    def plane_of(mine):
        return w.zh if mine else 1 - w.zh

    def load_weights():
        yield from plan.need()
        for copy in loads:
            copy.wait()
        plan.mark("weights")

    def side_rows():
        yield from plan.need(("r_n1", 1), ("r_dy", 1))
        spread_rows(side, r_n1[mate_low.here])
        spread_rows(side, r_dy[mate_high.here], SLOTS)
        plan.mark("side_rows")

    def first(mine):
        p = plane_of(mine)
        yield from plan.need((("n1", mine), 2), ("weights", 1))
        a = dot(n1[p].reshape(PLANE, WIDTH), wi[0])
        value, slope = gelu_both(a)
        u = value.astype(BF)
        slope1[p] = slope
        f_u1[index(mine)][w.core] = u
        for c in range(0, WIDTH, QUARTER):
            y = dot(u, wo[0, :, c : c + QUARTER]).astype(BF)
            part1[p, :, :, :, c : c + QUARTER] = y.reshape(4, 4, SLOTS, QUARTER)
        plan.work(2.0)
        plan.mark(("part1", mine))
        plan.mark("u1")

    def middle():
        yield from plan.need(("red1", 1))
        h = (x_own[...] + red1[5][...]).astype(BF).astype(F32)
        rows = norm_rows(h, gains[0, 1:2, :]).astype(BF)
        spread_rows(n2, rows)
        r_n2[w.core] = rows
        plan.work(0.6)
        plan.mark("n2_own")

    def pull(mine):
        p = plane_of(mine)
        yield from plan.need((("dy", mine), 2), ("weights", 1))
        pull2[p] = dot_t(dy[p].reshape(PLANE, WIDTH), wo[1])
        plan.work(0.8)
        plan.mark(("pull2", mine))

    def second(mine):
        p = plane_of(mine)
        yield from plan.need((("n2", mine), 2), (("pull2", mine), 1))
        a = dot(n2[p].reshape(PLANE, WIDTH), wi[1])
        value, slope = gelu_both(a)
        f_u2[index(mine)][w.core] = value.astype(BF)
        da = (pull2[p] * slope).astype(BF)
        f_a2[index(mine)][w.core] = da
        for c in range(0, WIDTH, QUARTER):
            y = dot_t(da, wi[1, c : c + QUARTER, :]).astype(BF)
            part2[p, :, :, :, c : c + QUARTER] = y.reshape(4, 4, SLOTS, QUARTER)
        plan.work(2.0)
        plan.mark(("part2", mine))
        plan.mark("u2")

    def side_n2():
        yield from plan.need(("r_n2", 1))
        spread_rows(n2q, r_n2[mate_high.here])
        plan.mark("n2q_own")

    def back():
        yield from plan.need(("red2", 1))
        h = (x_own[...] + red1[5][...]).astype(BF).astype(F32)
        grad = norm_pull(h, gains[0, 1:2, :], red2[5][...])
        rows = (dy_own[...] + grad).astype(BF)
        spread_rows(dh, rows)
        r_dh[w.core] = rows
        plan.work(0.8)
        plan.mark("dh_own")

    def side_dh():
        yield from plan.need(("r_dh", 1))
        spread_rows(dhq, r_dh[mate_low.here])
        plan.mark("dhq_own")

    def third(mine):
        p = plane_of(mine)
        yield from plan.need((("dh", mine), 2))
        du = dot_t(dh[p].reshape(PLANE, WIDTH), wo[0])
        f_a1[index(mine)][w.core] = (du * slope1[p]).astype(BF)
        plan.work(0.8)
        plan.mark(("a1", mine))

    def in_order(factor, k):
        near, far = factor[0][k], factor[1][k]
        swap = w.zh == 1
        top, bottom = jnp.where(swap, far, near), jnp.where(swap, near, far)
        return jnp.concatenate([top, bottom], axis=0).T

    def delta(out, level, k, own, mate, own_rows, mate_rows, own_needs, mate_needs, turned):
        def product(factor, rows, cols):
            return (-dot(factor, rows(cols)) * scale).astype(BF)

        def first_part():
            yield from plan.need(*own_needs)
            factor = in_order(own, w.core)
            for c in range(0, WIDTH, QUARTER):
                cols = slice(c, c + QUARTER)
                own_part[k, :, cols] = product(factor, own_rows, cols)
                plan.work(0.15)
                yield from plan.need()
            plan.mark(("delta", k))

        def second_part():
            yield from plan.need((("delta", k), 1), *mate_needs)
            factor = in_order(own, mate.here)
            for c in range(0, WIDTH, QUARTER):
                cols = slice(c, c + QUARTER)
                there = product(factor, mate_rows, cols).astype(F32)
                mean = ((own_part[k, :, cols].astype(F32) + there) * 0.5).astype(BF)
                if turned:
                    out[level, cols, :] = mean.T
                else:
                    out[level, :, cols] = mean
                plan.work(0.22)
                yield from plan.need()

        return [first_part(), second_part()]

    def of(ref):
        return lambda cols: ref[:, :, :, :, cols].reshape(ROWS, QUARTER)

    def of_side(k):
        return lambda cols: side[:, :, :, k * SLOTS : (k + 1) * SLOTS, cols].reshape(ROWS, QUARTER)

    def both(name):
        return [((name, True), 2), ((name, False), 2)]

    def spread(f, number, mates, name, after):
        for mine in (True, False):
            i = index(mine)

            def keep(value, i=i):
                f[i][4] = value

            yield path_fetch(
                w,
                plan,
                lambda k, i=i: f[i].at[k],
                lambda k, i=i: f[i][k],
                keep,
                (stage.at[number, i], late.at[number, i]),
                mates,
                name,
                [((after, mine), 1)],
            )

    def rows_over(ref, number, mates, name, after):
        def keep(value):
            ref[4] = value

        return path_fetch(
            w,
            plan,
            lambda k: ref.at[k],
            lambda k: ref[k],
            keep,
            (row_stage.at[number], row_late.at[number]),
            mates,
            name,
            after,
        )

    def parts(name):
        return [((name, True), 1), ((name, False), 1)]

    high_out = delta(
        d_out, 1, 0, f_u2, mate_high, of(dy), of_side(1),
        both("dy") + parts("part2"), [("f_u2", 2)] + both("side"), False,
    )
    high_in = delta(
        d_in, 1, 1, f_a2, mate_high, of(n2), of(n2q),
        both("n2") + parts("part2"), [("f_a2", 2)] + both("n2q"), True,
    )
    low_out = delta(
        d_out, 0, 2, f_u1, mate_low, of(dh), of(dhq),
        both("dh"), [("f_u1", 2)] + both("dhq"), False,
    )
    low_in = delta(
        d_in, 0, 3, f_a1, mate_low, of(n1), of_side(0),
        parts("a1"), [("f_a1", 2)] + both("side"), True,
    )
    groups = [
        ("load", [load_weights()]),
        ("n1", gather(w, plan, n1, "n1", [])),
        ("first", [first(True), first(False)]),
        ("red1", reduce(w, plan, part1, red1, "red1", "part1")),
        ("mid", [middle()]),
        ("n2", gather(w, plan, n2, "n2", [("n2_own", 1)])),
        ("second", [second(True), second(False)]),
        ("red2", reduce(w, plan, part2, red2, "red2", "part2")),
        ("back", [back()]),
        ("dh", gather(w, plan, dh, "dh", [("dh_own", 1)])),
        ("third", [third(True), third(False)]),
        ("r_dh", [rows_over(r_dh, 3, mate_low, "r_dh", [("dh_own", 1)]), side_dh()]),
        ("dhq", gather(w, plan, dhq, "dhq", [("dhq_own", 1)])),
        ("f_a1", spread(f_a1, 1, mate_low, "f_a1", "a1")),
        ("own", [low_out[0], low_in[0]]),
        ("end", [low_out[1], low_in[1]]),
        ("dy", gather(w, plan, dy, "dy", [])),
        ("pull", [pull(True), pull(False)]),
        ("r_dy", [rows_over(r_dy, 1, mate_high, "r_dy", [])]),
        ("r_n1", [rows_over(r_n1, 0, mate_low, "r_n1", []), side_rows()]),
        ("side", gather(w, plan, side, "side", [("side_rows", 1)])),
        ("f_u1", spread(f_u1, 0, mate_low, "f_u1", "part1")),
        ("r_n2", [rows_over(r_n2, 2, mate_high, "r_n2", [("n2_own", 1)]), side_n2()]),
        ("f_u2", spread(f_u2, 2, mate_high, "f_u2", "part2")),
        ("f_a2", spread(f_a2, 3, mate_high, "f_a2", "part2")),
        ("n2q", gather(w, plan, n2q, "n2q", [("n2q_own", 1)])),
        ("high", high_out + high_in),
    ]
    plan.run([LAGS.get(name, (0.0, 0.0)) + (t,) for name, tasks in groups for t in tasks])
    w.drain()


def step_call(tokens, routes, cotangent, gains, w_in, w_out, partners):
    anywhere = pl.BlockSpec(memory_space=pl.ANY)
    vmem = pl.BlockSpec(memory_space=pltpu.VMEM)

    def full(rows):
        return pltpu.VMEM((2, 4, 4, rows, WIDTH), BF)

    def by_path():
        return pltpu.VMEM((5, 2, SLOTS, WIDTH), BF)

    def factor():
        return pltpu.VMEM((5, PLANE, HIDDEN), BF)

    return pl.pallas_call(
        step_kernel,
        out_shape=[
            jax.ShapeDtypeStruct((2, WIDTH, HIDDEN), BF),
            jax.ShapeDtypeStruct((2, HIDDEN, WIDTH), BF),
        ],
        in_specs=[pl.BlockSpec(memory_space=pltpu.SMEM)] + [vmem] * 4 + [anywhere] * 2,
        out_specs=[vmem, vmem],
        scratch_shapes=[
            pltpu.VMEM((8, 2, 2, WIDTH), BF),
            pltpu.VMEM((2, 8, 2, 2, WIDTH), BF),
            pltpu.VMEM((2, SLOTS, WIDTH), F32),
            pltpu.VMEM((2, SLOTS, WIDTH), F32),
            pltpu.VMEM((2, WIDTH, HIDDEN), BF),
            pltpu.VMEM((2, HIDDEN, WIDTH), BF),
            full(SLOTS),
            full(SLOTS),
            full(SLOTS),
            full(SLOTS),
            full(2 * SLOTS),
            full(SLOTS),
            full(SLOTS),
            by_path(),
            by_path(),
            by_path(),
            by_path(),
            pltpu.VMEM((4, 2, SLOTS, WIDTH), BF),
            pltpu.VMEM((4, 2, SLOTS, WIDTH), BF),
            factor(),
            factor(),
            factor(),
            factor(),
            factor(),
            factor(),
            factor(),
            factor(),
            pltpu.VMEM((4, 2, PLANE, HIDDEN), BF),
            pltpu.VMEM((4, 2, PLANE, HIDDEN), BF),
            pltpu.VMEM((2, PLANE, HIDDEN), F32),
            pltpu.VMEM((2, PLANE, HIDDEN), F32),
            pltpu.VMEM((2, PLANE, HIDDEN), F32),
            pltpu.VMEM((4, HIDDEN, WIDTH), BF),
            full(SLOTS),
            full(SLOTS),
        ]
        + reduce_scratch()
        + reduce_scratch()
        + [
            pltpu.SemaphoreType.DMA((2,)),
            pltpu.SemaphoreType.DMA((COPIES,)),
            pltpu.SemaphoreType.DMA((COPIES,)),
        ],
        compiler_params=pltpu.CompilerParams(
            collective_id=0, has_side_effects=True, vmem_limit_bytes=62 << 20
        ),
    )(partners, tokens, routes, cotangent, gains, w_in, w_out)


def body(tokens, routes, cotangent, gains, w_in, w_out, partners):
    d_in, d_out = step_call(tokens, routes, cotangent, gains, w_in, w_out, partners)
    return d_in[None], d_out[None]


def solution(mesh):
    in_specs = (
        P(("path", "shard"), None),
        P(("path", "shard"), None),
        P(("path", "shard"), None),
        P("path", None, None),
        P("path", None, None, "shard"),
        P("path", None, "shard", None),
        P(),
    )
    out_specs = (P("path", None, None, "shard"), P("path", None, "shard", None))
    return jax.shard_map(body, mesh=mesh, in_specs=in_specs, out_specs=out_specs, check_vma=False)
```
